32 devices in a mesh: wide: 8 (over z, y), narrow: 4 (over x, core).
Axes of the slice: x: 2, y: 2, z: 4, core: 2. Of those that a mesh axis runs over, the one named last changes fastest.
Arguments:
- stem: float32 [2, 8, 4, 512, 128], P(None, 'wide', 'narrow'), may hold values from -6 to 6
- branches: float32 [3, 2, 512, 512], replicated, may hold values from -0.1875 to 0.1875
- mode_order: int32 [3, 9], replicated, may hold values from 0 to 8, each once within a row
Outputs:
- final_stem: float32 [2, 8, 4, 512, 128], P(None, 'wide', 'narrow')
The draws below stay inside these ranges and needn't reach their ends.
Inputs may be any that keep to these rules, and one draw needn't show every extreme that they name: Each row of mode_order names every mode of 0 to 8 once.
All inputs are finite; a program needn't handle non-finite values.
Results may differ from the reference program's by a relative error of at most 0.0003.
Values may be sent and summed in bfloat16 or wider, within the bound.
No kernel may reach another device: no remote copies, remote signals or barrier semaphores. Data moves between devices by JAX's collectives and lax.ppermute only.
A program may use at most 64 MiB of HBM per device.

```python
import jax
import jax.numpy as jnp
from jax import lax

MODES = 9
COLUMNS = 512
STEM_ROWS = 128
WIDE_BLOCKS = 8
NARROW_BLOCKS = 4
STEPS = 3


def block_scale(key, extent, cuts, low, largest):
    gain = 1.0
    for position, blocks in cuts:
        steps = jax.random.uniform(jax.random.fold_in(jax.random.fold_in(key, 6), position), (blocks,), jnp.float32, low / len(cuts), largest / len(cuts))
        gain = gain * jnp.repeat(jnp.exp(steps), extent[position] // blocks).reshape((-1,) + (1,) * (len(extent) - 1 - position))
    return gain


def bell_draw(key, shape, width, limit, pieces=(), kind=jnp.bfloat16):
    loudness = block_scale(key, shape, pieces, -0.22, 0.18) if pieces else 1.0
    drawn = jax.random.normal(key, shape, jnp.float32) * width * loudness
    return jnp.minimum(jnp.maximum(drawn, -limit), limit).astype(kind)


def setup_inputs(seed: int = 0) -> dict:
    splits = jax.random.split(jax.random.key(seed), 4)
    return {
        "stem": bell_draw(splits[0], (2, WIDE_BLOCKS, NARROW_BLOCKS, COLUMNS, STEM_ROWS), 1.0, 6.0, ((1, 8), (2, 4)), jnp.float32),
        "branches": bell_draw(splits[1], (STEPS, 2, COLUMNS, COLUMNS), (2 * COLUMNS) ** -0.5, 0.1875, (), jnp.float32),
        "mode_order": jax.vmap(lambda own: jax.random.permutation(own, MODES))(jax.random.split(splits[2], STEPS)).reshape((STEPS, MODES)).astype(jnp.int32),
    }


def split_pair(values):
    high = values.astype(jnp.bfloat16)
    held = lax.optimization_barrier(high)
    low = (values - held.astype(jnp.float32)).astype(jnp.bfloat16)
    return high, low


def expand_order(order):
    column = jnp.arange(COLUMNS, dtype=jnp.int32)
    places = jnp.arange(MODES, dtype=jnp.int32)
    bits = jnp.bitwise_and(jnp.right_shift(column[:, None], places[None, :]), 1)
    return jnp.sum(jnp.left_shift(bits, order[None, :].astype(jnp.int32)), axis=1).astype(jnp.int32)


def mult(left, right):
    return jnp.einsum("jk,njr->nkr", left.astype(jnp.float32), right.astype(jnp.float32), precision=lax.Precision.HIGHEST)


def product(branch_pair, stem_pair):
    return mult(branch_pair[0], stem_pair[0]) + mult(branch_pair[0], stem_pair[1]) + mult(branch_pair[1], stem_pair[0])


def contract_block(block, branch_step, order):
    permuted = jnp.take(branch_step, expand_order(order), axis=1)
    bhigh, blow = split_pair(permuted)
    shigh, slow = split_pair(block)
    b_real, b_imag = (bhigh[0], blow[0]), (bhigh[1], blow[1])
    s_real, s_imag = (shigh[0], slow[0]), (shigh[1], slow[1])
    real = product(b_real, s_real) - product(b_imag, s_imag)
    imag = product(b_real, s_imag) + product(b_imag, s_real)
    return jnp.stack([real, imag])


def contract_all(tensor, branch_step, order):
    blocks = jnp.moveaxis(tensor, 1, 0)
    done = lax.map(lambda block: contract_block(block, branch_step, order), blocks)
    return jnp.moveaxis(done, 0, 1)


def reference(stem, branches, mode_order):
    wide_n = WIDE_BLOCKS
    narrow_n = NARROW_BLOCKS
    first = contract_all(stem, branches[0], mode_order[0])
    shaped = first.reshape(2, wide_n, narrow_n, narrow_n, COLUMNS // narrow_n, STEM_ROWS)
    swapped_one = jnp.transpose(shaped, (0, 1, 3, 2, 4, 5)).reshape(2, wide_n, narrow_n, COLUMNS, STEM_ROWS)
    second = contract_all(swapped_one, branches[1], mode_order[1])
    shaped = second.reshape(2, wide_n, narrow_n, wide_n, COLUMNS // wide_n, STEM_ROWS)
    swapped_two = jnp.transpose(shaped, (0, 3, 2, 1, 4, 5)).reshape(2, wide_n, narrow_n, COLUMNS, STEM_ROWS)
    return contract_all(swapped_two, branches[2], mode_order[2])
```

```python
import functools

import jax
import jax.numpy as jnp
from jax import lax
from jax.experimental import pallas as pl
from jax.experimental.pallas import tpu as pltpu
from jax.sharding import PartitionSpec as P

LANES = 128
SUBLANES = 8
TOP = 32767.0
FINE = 65536.0


def split_pair(values):
    high = values.astype(jnp.bfloat16)
    low = (values - high.astype(jnp.float32)).astype(jnp.bfloat16)
    return high, low


def dot(left, right):
    return lax.dot_general(left, right, (((1,), (0,)), ((), ())), preferred_element_type=jnp.float32)


def one_hot(order_ref, step, columns):
    row = lax.broadcasted_iota(jnp.int32, (SUBLANES, columns), 1)
    meets = jnp.zeros_like(row)
    for b in range(order_ref.shape[1]):
        bit = jnp.bitwise_and(jnp.right_shift(row, order_ref[step, b]), 1)
        meets = meets + jnp.left_shift(bit, b)
    column = lax.broadcasted_iota(jnp.int32, (columns, columns), 0)
    return jnp.where(column == meets[0:1, :], 1.0, 0.0).astype(jnp.bfloat16)


def fetch(step, branches_ref, held, sems):
    parts = held.shape[0]
    size = held.shape[2]
    copies = []
    for p in range(parts):
        copy = pltpu.make_async_copy(
            branches_ref.at[step, :, pl.ds(p * size, size), :], held.at[p], sems.at[p]
        )
        copy.start()
        copies.append(copy)
    return copies


def contract(order_ref, step, real, imag, held, copies):
    rows, columns = real.shape
    real_high, real_low = split_pair(real)
    imag_high, imag_low = split_pair(imag)
    pieces = jnp.concatenate([real_high, imag_high, real_low, imag_low], axis=0)
    moved = dot(pieces, one_hot(order_ref, step, columns)).astype(jnp.bfloat16)
    real_high, imag_high, real_low, imag_low = (moved[q * rows : (q + 1) * rows] for q in range(4))
    plain = jnp.concatenate([real_high, imag_high, real_low, imag_low], axis=0)
    turned = jnp.concatenate([-imag_high, real_high, -imag_low, real_low], axis=0)
    size = held.shape[2]
    wide_sum = jnp.zeros((4 * rows, columns), jnp.float32)
    high_sum = jnp.zeros((2 * rows, columns), jnp.float32)
    for p, copy in enumerate(copies):
        copy.wait()
        part = slice(p * size, (p + 1) * size)
        r_high, r_low = split_pair(held[p, 0])
        i_high, i_low = split_pair(held[p, 1])
        wide_sum = wide_sum + dot(plain[:, part], r_high) + dot(turned[:, part], i_high)
        high_sum = high_sum + dot(plain[: 2 * rows, part], r_low) + dot(turned[: 2 * rows, part], i_low)
    return wide_sum[: 2 * rows] + wide_sum[2 * rows :] + high_sum


def lane_block(shape, width):
    return lax.broadcasted_iota(jnp.int32, shape, 1) // width


def rotate(values, amount):
    amount = amount % LANES
    return pltpu.roll(values, amount, 1) if amount else values


def encode(out_ref, slot, real, imag):
    rows = real.shape[0]
    tall = jnp.maximum(jnp.abs(real), jnp.abs(imag)).reshape(rows // SUBLANES, SUBLANES, LANES)
    largest = jnp.maximum(jnp.max(tall, axis=0), 1e-30)
    level = jnp.ceil(jnp.log2(largest) * FINE)
    gain = jnp.exp2(level * (-1.0 / FINE)) * (TOP - 1.0)
    gain = jnp.broadcast_to(gain[None], tall.shape).reshape(rows, LANES)
    upper = jnp.round(real * gain).astype(jnp.int32)
    lower = jnp.round(imag * gain).astype(jnp.int32)
    out_ref[slot, 0:rows, :] = jnp.bitwise_or(jnp.left_shift(upper, 16), jnp.bitwise_and(lower, 0xFFFF))
    out_ref[slot, rows : rows + SUBLANES, :] = level.astype(jnp.int32)


def decode(in_ref, slot):
    rows = in_ref.shape[1] - SUBLANES
    codes = in_ref[slot, 0:rows, :]
    level = in_ref[slot, rows : rows + SUBLANES, :].astype(jnp.float32)
    step = jnp.exp2(level * (1.0 / FINE)) * (1.0 / (TOP - 1.0))
    step = jnp.broadcast_to(step[None], (rows // SUBLANES, SUBLANES, LANES)).reshape(rows, LANES)
    real = jnp.right_shift(codes, 16).astype(jnp.float32) * step
    imag = jnp.right_shift(jnp.left_shift(codes, 16), 16).astype(jnp.float32) * step
    return real, imag


def pack(out_ref, sums):
    blocks = out_ref.shape[0]
    rows = sums.shape[0] // 2
    width = sums.shape[1] // blocks
    share = LANES // width
    height = rows // share
    for tile in range(sums.shape[1] // LANES):
        lanes = slice(tile * LANES, (tile + 1) * LANES)
        both = (sums[:rows, lanes], sums[rows:, lanes])
        for p in range(share):
            made = []
            for values in both:
                piece = rotate(values[0:height], -p * width)
                for q in range(1, share):
                    other = rotate(values[q * height : (q + 1) * height], (q - p) * width)
                    piece = jnp.where(lane_block(other.shape, width) == q, other, piece)
                made.append(piece)
            encode(out_ref, tile * share + p, *made)


def unpack(in_ref, rows, columns):
    blocks = in_ref.shape[0]
    width = columns // blocks
    share = LANES // width
    tiles = []
    for tile in range(columns // LANES):
        got = [decode(in_ref, tile * share + p) for p in range(share)]
        both = []
        for c in range(2):
            groups = []
            for q in range(share):
                piece = rotate(got[0][c], -q * width)
                for p in range(1, share):
                    other = rotate(got[p][c], (p - q) * width)
                    piece = jnp.where(lane_block(other.shape, width) == p, other, piece)
                groups.append(piece)
            both.append(jnp.concatenate(groups, axis=0) if share > 1 else groups[0])
        tiles.append(both)
    return tuple(jnp.concatenate([t[c] for t in tiles], axis=1) for c in range(2))


def first_kernel(order_ref, stem_ref, branches_ref, out_ref, held, sems):
    copies = fetch(0, branches_ref, held, sems)
    real, imag = stem_ref[0].T, stem_ref[1].T
    pack(out_ref, contract(order_ref, 0, real, imag, held, copies))


def middle_kernel(order_ref, in_ref, branches_ref, out_ref, held, sems):
    copies = fetch(1, branches_ref, held, sems)
    columns = held.shape[3]
    rows = (in_ref.shape[1] - SUBLANES) * in_ref.shape[0] * LANES // columns
    real, imag = unpack(in_ref, rows, columns)
    pack(out_ref, contract(order_ref, 1, real, imag, held, copies))


def last_kernel(order_ref, in_ref, branches_ref, out_ref, held, sems):
    copies = fetch(2, branches_ref, held, sems)
    columns = held.shape[3]
    rows = (in_ref.shape[1] - SUBLANES) * in_ref.shape[0] * LANES // columns
    real, imag = unpack(in_ref, rows, columns)
    sums = contract(order_ref, 2, real, imag, held, copies)
    out_ref[0] = sums[:rows].T
    out_ref[1] = sums[rows:].T


PARTS = 2


def call(kernel, out_shape, order, data, branches):
    columns = branches.shape[3]
    return pl.pallas_call(
        kernel,
        out_shape=out_shape,
        in_specs=[
            pl.BlockSpec(memory_space=pltpu.SMEM),
            pl.BlockSpec(memory_space=pltpu.VMEM),
            pl.BlockSpec(memory_space=pl.ANY),
        ],
        out_specs=pl.BlockSpec(memory_space=pltpu.VMEM),
        scratch_shapes=[
            pltpu.VMEM((PARTS, 2, columns // PARTS, columns), jnp.float32),
            pltpu.SemaphoreType.DMA((PARTS,)),
        ],
        compiler_params=pltpu.CompilerParams(vmem_limit_bytes=32 << 20),
    )(order, data, branches)


def body(stem, branches, mode_order):
    columns, rows = stem.shape[3:]
    local = stem.reshape(2, columns, rows)

    def coded(blocks):
        return jax.ShapeDtypeStruct((blocks, rows * columns // blocks // LANES + SUBLANES, LANES), jnp.int32)

    swap = functools.partial(lax.all_to_all, split_axis=0, concat_axis=0, tiled=True)
    first = call(first_kernel, coded(lax.axis_size("narrow")), mode_order, local, branches)
    first = swap(first, "narrow")
    second = call(middle_kernel, coded(lax.axis_size("wide")), mode_order, first, branches)
    second = swap(second, "wide")
    final = call(last_kernel, jax.ShapeDtypeStruct((2, columns, rows), jnp.float32), mode_order, second, branches)
    return final.reshape(2, 1, 1, columns, rows)


def solution(mesh):
    return jax.shard_map(
        body,
        mesh=mesh,
        in_specs=(P(None, "wide", "narrow", None, None), P(), P()),
        out_specs=P(None, "wide", "narrow", None, None),
        check_vma=False,
    )
```

```python
import functools

import jax
import jax.numpy as jnp
from jax import lax
from jax.experimental import pallas as pl
from jax.experimental.pallas import tpu as pltpu
from jax.sharding import PartitionSpec as P

LANES = 128
SUBLANES = 8
TOP = 32767.0
FINE = 65536.0


def split_pair(values):
    high = values.astype(jnp.bfloat16)
    low = (values - high.astype(jnp.float32)).astype(jnp.bfloat16)
    return high, low


def dot(left, right):
    return lax.dot_general(left, right, (((1,), (0,)), ((), ())), preferred_element_type=jnp.float32)


def one_hot(order_ref, step, columns):
    row = lax.broadcasted_iota(jnp.int32, (SUBLANES, columns), 1)
    meets = jnp.zeros_like(row)
    for b in range(order_ref.shape[1]):
        bit = jnp.bitwise_and(jnp.right_shift(row, order_ref[step, b]), 1)
        meets = meets + jnp.left_shift(bit, b)
    column = lax.broadcasted_iota(jnp.int32, (columns, columns), 0)
    return jnp.where(column == meets[0:1, :], 1.0, 0.0).astype(jnp.bfloat16)


def fetch(step, branches_ref, held, sems):
    parts = held.shape[0]
    size = held.shape[2]
    copies = []
    for p in range(parts):
        copy = pltpu.make_async_copy(
            branches_ref.at[step, :, pl.ds(p * size, size), :], held.at[p], sems.at[p]
        )
        copy.start()
        copies.append(copy)
    return copies


def contract(order_ref, step, real, imag, held, copies):
    rows, columns = real.shape
    real_high, real_low = split_pair(real)
    imag_high, imag_low = split_pair(imag)
    pieces = jnp.concatenate([real_high, imag_high, real_low, imag_low], axis=0)
    moved = dot(pieces, one_hot(order_ref, step, columns)).astype(jnp.bfloat16)
    real_high, imag_high, real_low, imag_low = (moved[q * rows : (q + 1) * rows] for q in range(4))
    plain = jnp.concatenate([real_high, imag_high, real_low, imag_low], axis=0)
    turned = jnp.concatenate([-imag_high, real_high, -imag_low, real_low], axis=0)
    size = held.shape[2]
    wide_sum = jnp.zeros((4 * rows, columns), jnp.float32)
    high_sum = jnp.zeros((2 * rows, columns), jnp.float32)
    for p, copy in enumerate(copies):
        copy.wait()
        part = slice(p * size, (p + 1) * size)
        r_high, r_low = split_pair(held[p, 0])
        i_high, i_low = split_pair(held[p, 1])
        wide_sum = wide_sum + dot(plain[:, part], r_high) + dot(turned[:, part], i_high)
        high_sum = high_sum + dot(plain[: 2 * rows, part], r_low) + dot(turned[: 2 * rows, part], i_low)
    return wide_sum[: 2 * rows] + wide_sum[2 * rows :] + high_sum


def lane_block(shape, width):
    return lax.broadcasted_iota(jnp.int32, shape, 1) // width


def rotate(values, amount):
    amount = amount % LANES
    return pltpu.roll(values, amount, 1) if amount else values


def encode(out_ref, slot, real, imag):
    rows = real.shape[0]
    tall = jnp.maximum(jnp.abs(real), jnp.abs(imag)).reshape(rows // SUBLANES, SUBLANES, LANES)
    largest = jnp.maximum(jnp.max(tall, axis=0), 1e-30)
    level = jnp.ceil(jnp.log2(largest) * FINE)
    gain = jnp.exp2(level * (-1.0 / FINE)) * (TOP - 1.0)
    gain = jnp.broadcast_to(gain[None], tall.shape).reshape(rows, LANES)
    upper = jnp.round(real * gain).astype(jnp.int32)
    lower = jnp.round(imag * gain).astype(jnp.int32)
    out_ref[slot, 0:rows, :] = jnp.bitwise_or(jnp.left_shift(upper, 16), jnp.bitwise_and(lower, 0xFFFF))
    out_ref[slot, rows : rows + SUBLANES, :] = level.astype(jnp.int32)


def decode(in_ref, slot):
    rows = in_ref.shape[1] - SUBLANES
    codes = in_ref[slot, 0:rows, :]
    level = in_ref[slot, rows : rows + SUBLANES, :].astype(jnp.float32)
    step = jnp.exp2(level * (1.0 / FINE)) * (1.0 / (TOP - 1.0))
    step = jnp.broadcast_to(step[None], (rows // SUBLANES, SUBLANES, LANES)).reshape(rows, LANES)
    real = jnp.right_shift(codes, 16).astype(jnp.float32) * step
    imag = jnp.right_shift(jnp.left_shift(codes, 16), 16).astype(jnp.float32) * step
    return real, imag


def pack(out_ref, sums):
    blocks = out_ref.shape[0]
    rows = sums.shape[0] // 2
    width = sums.shape[1] // blocks
    share = LANES // width
    height = rows // share
    for tile in range(sums.shape[1] // LANES):
        lanes = slice(tile * LANES, (tile + 1) * LANES)
        both = (sums[:rows, lanes], sums[rows:, lanes])
        for p in range(share):
            made = []
            for values in both:
                piece = rotate(values[0:height], -p * width)
                for q in range(1, share):
                    other = rotate(values[q * height : (q + 1) * height], (q - p) * width)
                    piece = jnp.where(lane_block(other.shape, width) == q, other, piece)
                made.append(piece)
            encode(out_ref, tile * share + p, *made)


def unpack(in_ref, rows, columns):
    blocks = in_ref.shape[0]
    width = columns // blocks
    share = LANES // width
    tiles = []
    for tile in range(columns // LANES):
        got = [decode(in_ref, tile * share + p) for p in range(share)]
        both = []
        for c in range(2):
            groups = []
            for q in range(share):
                piece = rotate(got[0][c], -q * width)
                for p in range(1, share):
                    other = rotate(got[p][c], (p - q) * width)
                    piece = jnp.where(lane_block(other.shape, width) == p, other, piece)
                groups.append(piece)
            both.append(jnp.concatenate(groups, axis=0) if share > 1 else groups[0])
        tiles.append(both)
    return tuple(jnp.concatenate([t[c] for t in tiles], axis=1) for c in range(2))


def exchange_ready(out_refs, chunks, axis):
    if len(out_refs) == 1:
        out_refs[0][...] = chunks[...]
        return
    me = lax.axis_index(axis)
    for s, ref in enumerate(out_refs):
        ref[...] = chunks[jnp.bitwise_xor(me, s)]


def exchange_done(in_refs, chunks, axis):
    if len(in_refs) == 1:
        chunks[...] = in_refs[0][...]
        return
    me = lax.axis_index(axis)
    for s, ref in enumerate(in_refs):
        chunks[jnp.bitwise_xor(me, s)] = ref[...]


def kernel(step, ins, outs, in_axis, out_axis, order_hbm, branches_hbm, *refs):
    in_refs, refs = refs[:ins], refs[ins:]
    out_refs, refs = refs[:outs], refs[outs:]
    order_ref, held, sems, ends, *chunks = refs
    copies = fetch(step, branches_hbm, held, sems)
    order_copy = pltpu.make_async_copy(order_hbm, order_ref, ends.at[0])
    order_copy.start()
    columns = held.shape[3]
    if in_axis is None:
        stem_ref = chunks.pop(0)
        stem_copy = pltpu.make_async_copy(in_refs[0], stem_ref, ends.at[1])
        stem_copy.start()
        stem_copy.wait()
        real, imag = stem_ref[0].T, stem_ref[1].T
    else:
        in_chunks = chunks.pop(0)
        exchange_done(in_refs, in_chunks, in_axis)
        rows = (in_chunks.shape[1] - SUBLANES) * in_chunks.shape[0] * LANES // columns
        real, imag = unpack(in_chunks, rows, columns)
    order_copy.wait()
    sums = contract(order_ref, step, real, imag, held, copies)
    if out_axis is None:
        rows = real.shape[0]
        out_refs[0][0] = sums[:rows].T
        out_refs[0][1] = sums[rows:].T
    else:
        out_chunks = chunks.pop(0)
        pack(out_chunks, sums)
        exchange_ready(out_refs, out_chunks, out_axis)


PARTS = 2
DIRECT = 8


def stage(step, mode_order, branches, ins, in_axis, out_axis, rows):
    columns = branches.shape[3]

    def chunks(axis):
        size = lax.axis_size(axis)
        return size, rows * columns // size // LANES + SUBLANES, LANES

    def split(axis):
        return lax.axis_size(axis) <= DIRECT

    if out_axis is None:
        out_shape = [jax.ShapeDtypeStruct((2, columns, rows), jnp.float32)]
    elif split(out_axis):
        shape = chunks(out_axis)
        out_shape = [jax.ShapeDtypeStruct(shape[1:], jnp.int32)] * shape[0]
    else:
        out_shape = [jax.ShapeDtypeStruct(chunks(out_axis), jnp.int32)]
    scratch = [
        pltpu.SMEM(mode_order.shape, jnp.int32),
        pltpu.VMEM((PARTS, 2, columns // PARTS, columns), jnp.float32),
        pltpu.SemaphoreType.DMA((PARTS,)),
        pltpu.SemaphoreType.DMA((2,)),
        pltpu.VMEM((2, columns, rows), jnp.float32) if in_axis is None else pltpu.VMEM(chunks(in_axis), jnp.int32),
    ]
    if out_axis is not None:
        scratch.append(pltpu.VMEM(chunks(out_axis), jnp.int32))
    hbm = pl.BlockSpec(memory_space=pltpu.HBM)
    vmem = pl.BlockSpec(memory_space=pltpu.VMEM)
    outs = pl.pallas_call(
        functools.partial(kernel, step, len(ins), len(out_shape), in_axis, out_axis),
        out_shape=out_shape,
        in_specs=[hbm, hbm] + [hbm if in_axis is None else vmem] * len(ins),
        out_specs=[vmem] * len(out_shape),
        scratch_shapes=scratch,
        compiler_params=pltpu.CompilerParams(vmem_limit_bytes=32 << 20),
    )(mode_order, branches, *ins)
    if out_axis is None:
        return outs[0]
    if len(outs) == 1:
        return [lax.all_to_all(outs[0], out_axis, split_axis=0, concat_axis=0, tiled=True)]
    size = lax.axis_size(out_axis)
    return list(outs[:1]) + [
        lax.ppermute(outs[s], out_axis, [(i, i ^ s) for i in range(size)]) for s in range(1, size)
    ]


def body(stem, branches, mode_order):
    columns, rows = stem.shape[3:]
    branches = pltpu.with_memory_space_constraint(branches, pltpu.HBM)
    mode_order = pltpu.with_memory_space_constraint(mode_order, pltpu.HBM)
    data = [pltpu.with_memory_space_constraint(stem.reshape(2, columns, rows), pltpu.HBM)]
    data = stage(0, mode_order, branches, data, None, "narrow", rows)
    data = stage(1, mode_order, branches, data, "narrow", "wide", rows)
    final = stage(2, mode_order, branches, data, "wide", None, rows)
    return final.reshape(2, 1, 1, columns, rows)


def solution(mesh):
    return jax.shard_map(
        body,
        mesh=mesh,
        in_specs=(P(None, "wide", "narrow", None, None), P(), P()),
        out_specs=P(None, "wide", "narrow", None, None),
        check_vma=False,
    )
```

```python
import functools

import jax
import jax.numpy as jnp
from jax import lax
from jax.experimental import pallas as pl
from jax.experimental.pallas import tpu as pltpu
from jax.sharding import PartitionSpec as P

LANES = 128
SUBLANES = 8
TOP = 32767.0
FINE = 65536.0


def split_pair(values):
    high = values.astype(jnp.bfloat16)
    low = (values - high.astype(jnp.float32)).astype(jnp.bfloat16)
    return high, low


def dot(left, right):
    return lax.dot_general(left, right, (((1,), (0,)), ((), ())), preferred_element_type=jnp.float32)


def one_hot(order_ref, step, columns):
    row = lax.broadcasted_iota(jnp.int32, (SUBLANES, columns), 1)
    meets = jnp.zeros_like(row)
    for b in range(order_ref.shape[1]):
        bit = jnp.bitwise_and(jnp.right_shift(row, order_ref[step, b]), 1)
        meets = meets + jnp.left_shift(bit, b)
    column = lax.broadcasted_iota(jnp.int32, (columns, columns), 0)
    return jnp.where(column == meets[0:1, :], 1.0, 0.0).astype(jnp.bfloat16)


def fetch(step, branches_ref, held, sems):
    parts = held.shape[0]
    size = held.shape[2]
    copies = []
    for p in range(parts):
        copy = pltpu.make_async_copy(
            branches_ref.at[step, :, pl.ds(p * size, size), :], held.at[p], sems.at[p]
        )
        copy.start()
        copies.append(copy)
    return copies


def contract(order_ref, step, real, imag, held, copies):
    rows, columns = real.shape
    real_high, real_low = split_pair(real)
    imag_high, imag_low = split_pair(imag)
    pieces = jnp.concatenate([real_high, imag_high, real_low, imag_low], axis=0)
    moved = dot(pieces, one_hot(order_ref, step, columns)).astype(jnp.bfloat16)
    real_high, imag_high, real_low, imag_low = (moved[q * rows : (q + 1) * rows] for q in range(4))
    plain = jnp.concatenate([real_high, imag_high, real_low, imag_low], axis=0)
    turned = jnp.concatenate([-imag_high, real_high, -imag_low, real_low], axis=0)
    size = held.shape[2]
    wide_sum = jnp.zeros((4 * rows, columns), jnp.float32)
    high_sum = jnp.zeros((2 * rows, columns), jnp.float32)
    for p, copy in enumerate(copies):
        copy.wait()
        part = slice(p * size, (p + 1) * size)
        r_high, r_low = split_pair(held[p, 0])
        i_high, i_low = split_pair(held[p, 1])
        wide_sum = wide_sum + dot(plain[:, part], r_high) + dot(turned[:, part], i_high)
        high_sum = high_sum + dot(plain[: 2 * rows, part], r_low) + dot(turned[: 2 * rows, part], i_low)
    return wide_sum[: 2 * rows] + wide_sum[2 * rows :] + high_sum


def lane_block(shape, width):
    return lax.broadcasted_iota(jnp.int32, shape, 1) // width


def rotate(values, amount):
    amount = amount % LANES
    return pltpu.roll(values, amount, 1) if amount else values


def encode(out_ref, slot, real, imag):
    rows = real.shape[0]
    tall = jnp.maximum(jnp.abs(real), jnp.abs(imag)).reshape(rows // SUBLANES, SUBLANES, LANES)
    largest = jnp.maximum(jnp.max(tall, axis=0), 1e-30)
    level = jnp.ceil(jnp.log2(largest) * FINE)
    gain = jnp.exp2(level * (-1.0 / FINE)) * (TOP - 1.0)
    gain = jnp.broadcast_to(gain[None], tall.shape).reshape(rows, LANES)
    upper = jnp.round(real * gain).astype(jnp.int32)
    lower = jnp.round(imag * gain).astype(jnp.int32)
    out_ref[slot, 0:rows, :] = jnp.bitwise_or(jnp.left_shift(upper, 16), jnp.bitwise_and(lower, 0xFFFF))
    out_ref[slot, rows : rows + SUBLANES, :] = level.astype(jnp.int32)


def decode(in_ref, slot):
    rows = in_ref.shape[1] - SUBLANES
    codes = in_ref[slot, 0:rows, :]
    level = in_ref[slot, rows : rows + SUBLANES, :].astype(jnp.float32)
    step = jnp.exp2(level * (1.0 / FINE)) * (1.0 / (TOP - 1.0))
    step = jnp.broadcast_to(step[None], (rows // SUBLANES, SUBLANES, LANES)).reshape(rows, LANES)
    real = jnp.right_shift(codes, 16).astype(jnp.float32) * step
    imag = jnp.right_shift(jnp.left_shift(codes, 16), 16).astype(jnp.float32) * step
    return real, imag


def pack(out_ref, sums):
    blocks = out_ref.shape[0]
    rows = sums.shape[0] // 2
    width = sums.shape[1] // blocks
    share = LANES // width
    height = rows // share
    for tile in range(sums.shape[1] // LANES):
        lanes = slice(tile * LANES, (tile + 1) * LANES)
        both = (sums[:rows, lanes], sums[rows:, lanes])
        for p in range(share):
            made = []
            for values in both:
                piece = rotate(values[0:height], -p * width)
                for q in range(1, share):
                    other = rotate(values[q * height : (q + 1) * height], (q - p) * width)
                    piece = jnp.where(lane_block(other.shape, width) == q, other, piece)
                made.append(piece)
            encode(out_ref, tile * share + p, *made)


def unpack(in_ref, rows, columns):
    blocks = in_ref.shape[0]
    width = columns // blocks
    share = LANES // width
    tiles = []
    for tile in range(columns // LANES):
        got = [decode(in_ref, tile * share + p) for p in range(share)]
        both = []
        for c in range(2):
            groups = []
            for q in range(share):
                piece = rotate(got[0][c], -q * width)
                for p in range(1, share):
                    other = rotate(got[p][c], (p - q) * width)
                    piece = jnp.where(lane_block(other.shape, width) == p, other, piece)
                groups.append(piece)
            both.append(jnp.concatenate(groups, axis=0) if share > 1 else groups[0])
        tiles.append(both)
    return tuple(jnp.concatenate([t[c] for t in tiles], axis=1) for c in range(2))


def partners(size):
    half = size // 2
    return [0] + sorted(range(1, size), key=lambda s: (s < half, -(s % 2), -s))


def exchange_ready(out_refs, chunks, axis):
    if len(out_refs) == 1:
        out_refs[0][...] = chunks[...]
        return
    me = lax.axis_index(axis)
    for s, ref in zip(partners(len(out_refs)), out_refs):
        ref[...] = chunks[jnp.bitwise_xor(me, s)]


def exchange_done(in_refs, chunks, axis):
    if len(in_refs) == 1:
        chunks[...] = in_refs[0][...]
        return
    me = lax.axis_index(axis)
    for s, ref in zip(partners(len(in_refs)), in_refs):
        chunks[jnp.bitwise_xor(me, s)] = ref[...]


def kernel(step, ins, outs, in_axis, out_axis, order_hbm, branches_hbm, *refs):
    in_refs, refs = refs[:ins], refs[ins:]
    out_refs, refs = refs[:outs], refs[outs:]
    order_ref, held, sems, ends, *chunks = refs
    order_copy = pltpu.make_async_copy(order_hbm, order_ref, ends.at[0])
    order_copy.start()
    if in_axis is None:
        stem_ref = chunks.pop(0)
        stem_copy = pltpu.make_async_copy(in_refs[0], stem_ref, ends.at[1])
        stem_copy.start()
    copies = fetch(step, branches_hbm, held, sems)
    columns = held.shape[3]
    if in_axis is None:
        stem_copy.wait()
        real, imag = stem_ref[0].T, stem_ref[1].T
    else:
        in_chunks = chunks.pop(0)
        exchange_done(in_refs, in_chunks, in_axis)
        rows = (in_chunks.shape[1] - SUBLANES) * in_chunks.shape[0] * LANES // columns
        real, imag = unpack(in_chunks, rows, columns)
    order_copy.wait()
    sums = contract(order_ref, step, real, imag, held, copies)
    if out_axis is None:
        rows = real.shape[0]
        out_refs[0][0] = sums[:rows].T
        out_refs[0][1] = sums[rows:].T
    else:
        out_chunks = chunks.pop(0)
        pack(out_chunks, sums)
        exchange_ready(out_refs, out_chunks, out_axis)


def swap(outs, axis):
    size = lax.axis_size(axis)
    order = partners(size)
    return list(outs[:1]) + [
        lax.ppermute(out, axis, [(i, i ^ s) for i in range(size)]) for s, out in zip(order[1:], outs[1:])
    ]


PARTS = 2
DIRECT = 8


def stage(step, mode_order, branches, ins, in_axis, out_axis, rows):
    columns = branches.shape[3]

    def chunks(axis):
        size = lax.axis_size(axis)
        return size, rows * columns // size // LANES + SUBLANES, LANES

    def split(axis):
        return lax.axis_size(axis) <= DIRECT

    if out_axis is None:
        out_shape = [jax.ShapeDtypeStruct((2, columns, rows), jnp.float32)]
    elif split(out_axis):
        shape = chunks(out_axis)
        out_shape = [jax.ShapeDtypeStruct(shape[1:], jnp.int32)] * shape[0]
    else:
        out_shape = [jax.ShapeDtypeStruct(chunks(out_axis), jnp.int32)]
    scratch = [
        pltpu.SMEM(mode_order.shape, jnp.int32),
        pltpu.VMEM((PARTS, 2, columns // PARTS, columns), jnp.float32),
        pltpu.SemaphoreType.DMA((PARTS,)),
        pltpu.SemaphoreType.DMA((2,)),
        pltpu.VMEM((2, columns, rows), jnp.float32) if in_axis is None else pltpu.VMEM(chunks(in_axis), jnp.int32),
    ]
    if out_axis is not None:
        scratch.append(pltpu.VMEM(chunks(out_axis), jnp.int32))
    hbm = pl.BlockSpec(memory_space=pltpu.HBM)
    vmem = pl.BlockSpec(memory_space=pltpu.VMEM)
    outs = pl.pallas_call(
        functools.partial(kernel, step, len(ins), len(out_shape), in_axis, out_axis),
        out_shape=out_shape,
        in_specs=[hbm, hbm] + [hbm if in_axis is None else vmem] * len(ins),
        out_specs=[vmem] * len(out_shape),
        scratch_shapes=scratch,
        compiler_params=pltpu.CompilerParams(vmem_limit_bytes=32 << 20),
    )(mode_order, branches, *ins)
    if out_axis is None:
        return outs[0]
    if len(outs) == 1:
        return [lax.all_to_all(outs[0], out_axis, split_axis=0, concat_axis=0, tiled=True)]
    return swap(outs, out_axis)


def body(stem, branches, mode_order):
    columns, rows = stem.shape[3:]
    branches = pltpu.with_memory_space_constraint(branches, pltpu.HBM)
    mode_order = pltpu.with_memory_space_constraint(mode_order, pltpu.HBM)
    data = [pltpu.with_memory_space_constraint(stem.reshape(2, columns, rows), pltpu.HBM)]
    data = stage(0, mode_order, branches, data, None, "narrow", rows)
    data = stage(1, mode_order, branches, data, "narrow", "wide", rows)
    final = stage(2, mode_order, branches, data, "wide", None, rows)
    return final.reshape(2, 1, 1, columns, rows)


def solution(mesh):
    return jax.shard_map(
        body,
        mesh=mesh,
        in_specs=(P(None, "wide", "narrow", None, None), P(), P()),
        out_specs=P(None, "wide", "narrow", None, None),
        check_vma=False,
    )
```

```python
import functools

import jax
import jax.numpy as jnp
from jax import lax
from jax.experimental import pallas as pl
from jax.experimental.pallas import tpu as pltpu
from jax.sharding import PartitionSpec as P

LANES = 128
SUBLANES = 8
TOP = 32766.0
FINE = 65536.0
HALVES = 2
DIRECT = 8
VMEM_LIMIT = 24 << 20


def split_pair(values):
    high = values.astype(jnp.bfloat16)
    low = (values - high.astype(jnp.float32)).astype(jnp.bfloat16)
    return high, low


def dot(left, right):
    return lax.dot_general(left, right, (((1,), (0,)), ((), ())), preferred_element_type=jnp.float32)


def one_hot(order_ref, step, columns):
    row = lax.broadcasted_iota(jnp.int32, (SUBLANES, columns), 1)
    meets = jnp.zeros_like(row)
    for b in range(order_ref.shape[1]):
        bit = jnp.bitwise_and(jnp.right_shift(row, order_ref[step, b]), 1)
        meets = meets + jnp.left_shift(bit, b)
    column = lax.broadcasted_iota(jnp.int32, (columns, columns), 0)
    return jnp.where(column == meets[0:1, :], 1.0, 0.0).astype(jnp.bfloat16)


def operands(pieces):
    real_high, imag_high, real_low, imag_low = pieces
    plain = jnp.concatenate([real_high, imag_high, real_low, imag_low], axis=0)
    turned = jnp.concatenate([-imag_high, real_high, -imag_low, real_low], axis=0)
    return plain, turned


def contract(plain, turned, branch):
    real_high, imag_high, real_low, imag_low = branch
    rows = plain.shape[0] // 2
    both = dot(plain, real_high) + dot(turned, imag_high)
    low = dot(plain[:rows], real_low) + dot(turned[:rows], imag_low)
    return both[:rows] + both[rows:] + low


def lane_block(shape, width):
    return lax.broadcasted_iota(jnp.int32, shape, 1) // width


def rotate(values, amount):
    amount = amount % LANES
    return pltpu.roll(values, amount, 1) if amount else values


def encode(out_ref, slot, real, imag):
    rows = real.shape[0]
    tall = jnp.maximum(jnp.abs(real), jnp.abs(imag)).reshape(rows // SUBLANES, SUBLANES, LANES)
    largest = jnp.maximum(jnp.max(tall, axis=0), 1e-30)
    level = jnp.ceil(jnp.log2(largest) * FINE)
    gain = jnp.exp2(level * (-1.0 / FINE)) * TOP
    gain = jnp.broadcast_to(gain[None], tall.shape).reshape(rows, LANES)
    upper = jnp.round(real * gain).astype(jnp.int32)
    lower = jnp.round(imag * gain).astype(jnp.int32)
    out_ref[slot, 0:rows, :] = jnp.bitwise_or(jnp.left_shift(upper, 16), jnp.bitwise_and(lower, 0xFFFF))
    out_ref[slot, rows : rows + SUBLANES, :] = level.astype(jnp.int32)


def decode(in_ref, slot):
    rows = in_ref.shape[1] - SUBLANES
    codes = in_ref[slot, 0:rows, :]
    level = in_ref[slot, rows : rows + SUBLANES, :].astype(jnp.float32)
    step = jnp.exp2(level * (1.0 / FINE)) * (1.0 / TOP)
    step = jnp.broadcast_to(step[None], (rows // SUBLANES, SUBLANES, LANES)).reshape(rows, LANES)
    real = jnp.right_shift(codes, 16).astype(jnp.float32) * step
    imag = jnp.right_shift(jnp.left_shift(codes, 16), 16).astype(jnp.float32) * step
    return real, imag


def pack(out_ref, tile, width, real, imag):
    share = LANES // width
    height = real.shape[0] // share
    for p in range(share):
        made = []
        for values in (real, imag):
            piece = rotate(values[0:height], -p * width)
            for q in range(1, share):
                other = rotate(values[q * height : (q + 1) * height], (q - p) * width)
                piece = jnp.where(lane_block(other.shape, width) == q, other, piece)
            made.append(piece)
        encode(out_ref, tile * share + p, *made)


def unpack(in_ref, columns):
    blocks = in_ref.shape[0]
    width = columns // blocks
    share = LANES // width
    tiles = []
    for tile in range(columns // LANES):
        got = [decode(in_ref, tile * share + p) for p in range(share)]
        both = []
        for c in range(2):
            groups = []
            for q in range(share):
                piece = rotate(got[0][c], -q * width)
                for p in range(1, share):
                    other = rotate(got[p][c], (p - q) * width)
                    piece = jnp.where(lane_block(other.shape, width) == p, other, piece)
                groups.append(piece)
            both.append(jnp.concatenate(groups, axis=0) if share > 1 else groups[0])
        tiles.append(both)
    return tuple(jnp.concatenate([t[c] for t in tiles], axis=1) for c in range(2))


def partners(size):
    half = size // 2
    return [0] + sorted(range(1, size), key=lambda s: (s < half, -(s % 2), -s))


def exchange_ready(out_refs, chunks, axis):
    if len(out_refs) == 1:
        out_refs[0][...] = chunks[...]
        return
    me = lax.axis_index(axis)
    for s, ref in zip(partners(len(out_refs)), out_refs):
        ref[...] = chunks[jnp.bitwise_xor(me, s)]


def exchange_done(in_refs, chunks, axis):
    if len(in_refs) == 1:
        chunks[...] = in_refs[0][...]
        return
    me = lax.axis_index(axis)
    for s, ref in zip(partners(len(in_refs)), in_refs):
        chunks[jnp.bitwise_xor(me, s)] = ref[...]


def first_kernel(axis, order_hbm, stem_hbm, branches_hbm, *refs):
    *out_refs, next_ref, order_ref, stem_ref, held, chunks, sems = refs
    columns = held.shape[2]
    part = held.shape[3]
    width = columns // chunks.shape[0]
    order_copy = pltpu.make_async_copy(order_hbm, order_ref, sems.at[0])
    stem_copy = pltpu.make_async_copy(stem_hbm, stem_ref, sems.at[1])
    next_copy = pltpu.make_async_copy(branches_hbm.at[1], next_ref, sems.at[2])
    copies = [
        pltpu.make_async_copy(branches_hbm.at[0, :, :, pl.ds(h * part, part)], held.at[h], sems.at[3 + h])
        for h in range(HALVES)
    ]
    for copy in [order_copy, stem_copy, *copies, next_copy]:
        copy.start()
    order_copy.wait()
    meets = one_hot(order_ref, 0, columns)
    stem_copy.wait()
    real_high, real_low = split_pair(stem_ref[0].T)
    imag_high, imag_low = split_pair(stem_ref[1].T)
    rows = real_high.shape[0]
    moved = dot(jnp.concatenate([real_high, imag_high, real_low, imag_low], axis=0), meets).astype(jnp.bfloat16)
    plain, turned = operands([moved[q * rows : (q + 1) * rows] for q in range(4)])
    for h, copy in enumerate(copies):
        copy.wait()
        r_high, r_low = split_pair(held[h, 0])
        i_high, i_low = split_pair(held[h, 1])
        sums = contract(plain, turned, (r_high, i_high, r_low, i_low))
        for tile in range(part // LANES):
            lanes = slice(tile * LANES, (tile + 1) * LANES)
            pack(chunks, h * (part // LANES) + tile, width, sums[:rows, lanes], sums[rows:, lanes])
    exchange_ready(out_refs, chunks, axis)
    next_copy.wait()


def prepare_kernel(order_hbm, next_ref, branches_hbm, second_ref, third_ref, order_ref, held, sems):
    columns = next_ref.shape[1]
    order_copy = pltpu.make_async_copy(order_hbm, order_ref, sems.at[0])
    copy = pltpu.make_async_copy(branches_hbm.at[2], held, sems.at[1])
    order_copy.start()
    copy.start()
    order_copy.wait()
    for step, from_ref, to_ref in ((1, next_ref, second_ref), (2, held, third_ref)):
        meets = one_hot(order_ref, step, columns)
        if step == 2:
            copy.wait()
        for c in range(2):
            high, low = split_pair(from_ref[c])
            to_ref[c] = dot(meets, high).astype(jnp.bfloat16)
            to_ref[2 + c] = dot(meets, low).astype(jnp.bfloat16)


def received(in_refs, chunks, axis, columns):
    exchange_done(in_refs, chunks, axis)
    real, imag = unpack(chunks, columns)
    real_high, real_low = split_pair(real)
    imag_high, imag_low = split_pair(imag)
    return operands((real_high, imag_high, real_low, imag_low))


def middle_kernel(ins, in_axis, out_axis, branch_ref, *refs):
    in_refs, out_refs = refs[:ins], refs[ins:-2]
    arrived, chunks = refs[-2:]
    columns = branch_ref.shape[2]
    part = columns // HALVES
    width = columns // chunks.shape[0]
    plain, turned = received(in_refs, arrived, in_axis, columns)
    rows = plain.shape[0] // 4
    for h in range(HALVES):
        cut = slice(h * part, (h + 1) * part)
        sums = contract(plain, turned, [branch_ref[q, :, cut] for q in range(4)])
        for tile in range(part // LANES):
            lanes = slice(tile * LANES, (tile + 1) * LANES)
            pack(chunks, h * (part // LANES) + tile, width, sums[:rows, lanes], sums[rows:, lanes])
    exchange_ready(out_refs, chunks, out_axis)


def last_kernel(ins, in_axis, branch_ref, *refs):
    in_refs = refs[:ins]
    out_hbm, arrived, done, sems = refs[ins:]
    columns = branch_ref.shape[2]
    part = columns // HALVES
    plain, turned = received(in_refs, arrived, in_axis, columns)
    rows = plain.shape[0] // 4
    copies = []
    for h in range(HALVES):
        cut = slice(h * part, (h + 1) * part)
        sums = contract(plain, turned, [branch_ref[q, :, cut] for q in range(4)])
        done[h, 0] = sums[:rows].T
        done[h, 1] = sums[rows:].T
        copy = pltpu.make_async_copy(done.at[h], out_hbm.at[:, pl.ds(h * part, part), :], sems.at[h])
        copy.start()
        copies.append(copy)
    for copy in copies:
        copy.wait()


def swap(outs, axis):
    size = lax.axis_size(axis)
    if size > DIRECT:
        return [lax.all_to_all(outs[0], axis, split_axis=0, concat_axis=0, tiled=True)]
    order = partners(size)
    return list(outs[:1]) + [
        lax.ppermute(out, axis, [(i, i ^ s) for i in range(size)]) for s, out in zip(order[1:], outs[1:])
    ]


HBM = pl.BlockSpec(memory_space=pltpu.HBM)
VMEM = pl.BlockSpec(memory_space=pltpu.VMEM)


def call(kernel, out_shape, in_specs, out_specs, scratch, flops, args):
    params = pltpu.CompilerParams(vmem_limit_bytes=VMEM_LIMIT)
    cost = pl.CostEstimate(flops=flops, bytes_accessed=4 << 20, transcendentals=0)
    return pl.pallas_call(
        kernel, out_shape=out_shape, in_specs=in_specs, out_specs=out_specs, scratch_shapes=scratch,
        compiler_params=params, cost_estimate=cost,
    )(*args)


def body(stem, branches, mode_order):
    columns, rows = stem.shape[3:]
    part = columns // HALVES

    def block(axis):
        size = lax.axis_size(axis)
        return size, rows * columns // size // LANES + SUBLANES, LANES

    def coded(axis):
        shape = block(axis)
        if shape[0] > DIRECT:
            return [jax.ShapeDtypeStruct(shape, jnp.int32)]
        return [jax.ShapeDtypeStruct(shape[1:], jnp.int32)] * shape[0]

    def arrays(axis):
        return pltpu.VMEM(block(axis), jnp.int32)

    branches = pltpu.with_memory_space_constraint(branches, pltpu.HBM)
    mode_order = pltpu.with_memory_space_constraint(mode_order, pltpu.HBM)
    local = pltpu.with_memory_space_constraint(stem.reshape(2, columns, rows), pltpu.HBM)
    order = pltpu.SMEM(mode_order.shape, jnp.int32)
    product = 24 * rows * columns * columns

    shapes = coded("narrow")
    *outs, second_branch = call(
        functools.partial(first_kernel, "narrow"),
        shapes + [jax.ShapeDtypeStruct(branches.shape[1:], jnp.float32)],
        [HBM] * 3, [VMEM] * (len(shapes) + 1),
        [order, pltpu.VMEM(local.shape, jnp.float32), pltpu.VMEM((HALVES, 2, columns, part), jnp.float32),
         arrays("narrow"), pltpu.SemaphoreType.DMA((3 + HALVES,))],
        product, (mode_order, local, branches))
    ready = jax.ShapeDtypeStruct((4, columns, columns), jnp.bfloat16)
    second_branch, third_branch = call(
        prepare_kernel, [ready, ready], [HBM, VMEM, HBM], [VMEM, VMEM],
        [order, pltpu.VMEM(branches.shape[1:], jnp.float32), pltpu.SemaphoreType.DMA((2,))],
        16 * columns**3, (mode_order, second_branch, branches))
    outs = swap(outs, "narrow")
    shapes = coded("wide")
    outs = call(
        functools.partial(middle_kernel, len(outs), "narrow", "wide"), shapes,
        [VMEM] * (1 + len(outs)), [VMEM] * len(shapes), [arrays("narrow"), arrays("wide")],
        product, (second_branch, *outs))
    outs = swap(outs, "wide")
    final = call(
        functools.partial(last_kernel, len(outs), "wide"), jax.ShapeDtypeStruct((2, columns, rows), jnp.float32),
        [VMEM] * (1 + len(outs)), HBM,
        [arrays("wide"), pltpu.VMEM((HALVES, 2, part, rows), jnp.float32), pltpu.SemaphoreType.DMA((HALVES,))],
        product, (third_branch, *outs))
    return final.reshape(2, 1, 1, columns, rows)


def solution(mesh):
    return jax.shard_map(
        body,
        mesh=mesh,
        in_specs=(P(None, "wide", "narrow", None, None), P(), P()),
        out_specs=P(None, "wide", "narrow", None, None),
        check_vma=False,
    )
```

```python
import functools

import jax
import jax.numpy as jnp
from jax import lax
from jax.experimental import pallas as pl
from jax.experimental.pallas import tpu as pltpu
from jax.sharding import PartitionSpec as P

LANES = 128
SUBLANES = 8
TOP = 32766.0
FINE = 65536.0
HALVES = 2
PARTS = 4
DIRECT = 8
VMEM_LIMIT = 24 << 20


def split_pair(values):
    high = values.astype(jnp.bfloat16)
    low = (values - high.astype(jnp.float32)).astype(jnp.bfloat16)
    return high, low


def dot(left, right):
    return lax.dot_general(left, right, (((1,), (0,)), ((), ())), preferred_element_type=jnp.float32)


def one_hot(order_ref, step, columns):
    row = lax.broadcasted_iota(jnp.int32, (SUBLANES, columns), 1)
    meets = jnp.zeros_like(row)
    for b in range(order_ref.shape[1]):
        bit = jnp.bitwise_and(jnp.right_shift(row, order_ref[step, b]), 1)
        meets = meets + jnp.left_shift(bit, b)
    column = lax.broadcasted_iota(jnp.int32, (columns, columns), 0)
    return jnp.where(column == meets[0:1, :], 1.0, 0.0).astype(jnp.bfloat16)


def operands(pieces):
    real_high, imag_high, real_low, imag_low = pieces
    plain = jnp.concatenate([real_high, imag_high, real_low, imag_low], axis=0)
    turned = jnp.concatenate([-imag_high, real_high, -imag_low, real_low], axis=0)
    return plain, turned


def contract(plain, turned, branch):
    real_high, imag_high, real_low, imag_low = branch
    rows = plain.shape[0] // 2
    both = dot(plain, real_high) + dot(turned, imag_high)
    low = dot(plain[:rows], real_low) + dot(turned[:rows], imag_low)
    return both[:rows] + both[rows:] + low


def lane_block(shape, width):
    return lax.broadcasted_iota(jnp.int32, shape, 1) // width


def rotate(values, amount):
    amount = amount % LANES
    return pltpu.roll(values, amount, 1) if amount else values


def encode(out_ref, slot, real, imag):
    rows = real.shape[0]
    tall = jnp.maximum(jnp.abs(real), jnp.abs(imag)).reshape(rows // SUBLANES, SUBLANES, LANES)
    largest = jnp.maximum(jnp.max(tall, axis=0), 1e-30)
    level = jnp.ceil(jnp.log2(largest) * FINE)
    gain = jnp.exp2(level * (-1.0 / FINE)) * TOP
    gain = jnp.broadcast_to(gain[None], tall.shape).reshape(rows, LANES)
    upper = jnp.round(real * gain).astype(jnp.int32)
    lower = jnp.round(imag * gain).astype(jnp.int32)
    out_ref[slot, 0:rows, :] = jnp.bitwise_or(jnp.left_shift(upper, 16), jnp.bitwise_and(lower, 0xFFFF))
    out_ref[slot, rows : rows + SUBLANES, :] = level.astype(jnp.int32)


def decode(in_ref, slot):
    rows = in_ref.shape[1] - SUBLANES
    codes = in_ref[slot, 0:rows, :]
    level = in_ref[slot, rows : rows + SUBLANES, :].astype(jnp.float32)
    step = jnp.exp2(level * (1.0 / FINE)) * (1.0 / TOP)
    step = jnp.broadcast_to(step[None], (rows // SUBLANES, SUBLANES, LANES)).reshape(rows, LANES)
    real = jnp.right_shift(codes, 16).astype(jnp.float32) * step
    imag = jnp.right_shift(jnp.left_shift(codes, 16), 16).astype(jnp.float32) * step
    return real, imag


def pack(out_ref, tile, width, real, imag):
    share = LANES // width
    height = real.shape[0] // share
    for p in range(share):
        made = []
        for values in (real, imag):
            piece = rotate(values[0:height], -p * width)
            for q in range(1, share):
                other = rotate(values[q * height : (q + 1) * height], (q - p) * width)
                piece = jnp.where(lane_block(other.shape, width) == q, other, piece)
            made.append(piece)
        encode(out_ref, tile * share + p, *made)


def unpack(in_ref, columns):
    blocks = in_ref.shape[0]
    width = columns // blocks
    share = LANES // width
    tiles = []
    for tile in range(columns // LANES):
        got = [decode(in_ref, tile * share + p) for p in range(share)]
        both = []
        for c in range(2):
            groups = []
            for q in range(share):
                piece = rotate(got[0][c], -q * width)
                for p in range(1, share):
                    other = rotate(got[p][c], (p - q) * width)
                    piece = jnp.where(lane_block(other.shape, width) == p, other, piece)
                groups.append(piece)
            both.append(jnp.concatenate(groups, axis=0) if share > 1 else groups[0])
        tiles.append(both)
    return tuple(jnp.concatenate([t[c] for t in tiles], axis=1) for c in range(2))


def partners(size):
    half = size // 2
    return [0] + sorted(range(1, size), key=lambda s: (s < half, -(s % 2), -s))


def partners_near(size):
    return [s for s in partners(size) if s < size // 2]


def partners_far(size):
    return [s for s in partners(size) if s >= size // 2]


def exchange_ready(out_refs, chunks, axis):
    if len(out_refs) == 1:
        out_refs[0][...] = chunks[...]
        return
    me = lax.axis_index(axis)
    for s, ref in zip(partners(len(out_refs)), out_refs):
        ref[...] = chunks[jnp.bitwise_xor(me, s)]


def first_kernel(axis, order_hbm, stem_hbm, branches_hbm, *refs):
    *out_refs, order_ref, stem_ref, held, chunks, sems = refs
    parts, _, part, columns = held.shape
    width = columns // chunks.shape[0]
    order_copy = pltpu.make_async_copy(order_hbm, order_ref, sems.at[0])
    stem_copy = pltpu.make_async_copy(stem_hbm, stem_ref, sems.at[1])
    copies = [
        pltpu.make_async_copy(branches_hbm.at[0, :, pl.ds(p * part, part), :], held.at[p], sems.at[2 + p])
        for p in range(parts)
    ]
    for copy in [order_copy, stem_copy, *copies]:
        copy.start()
    order_copy.wait()
    meets = one_hot(order_ref, 0, columns)
    stem_copy.wait()
    real_high, real_low = split_pair(stem_ref[0].T)
    imag_high, imag_low = split_pair(stem_ref[1].T)
    rows = real_high.shape[0]
    moved = dot(jnp.concatenate([real_high, imag_high, real_low, imag_low], axis=0), meets).astype(jnp.bfloat16)
    plain, turned = operands([moved[q * rows : (q + 1) * rows] for q in range(4)])
    both = jnp.zeros((4 * rows, columns), jnp.float32)
    low = jnp.zeros((2 * rows, columns), jnp.float32)
    for p, copy in enumerate(copies):
        copy.wait()
        cut = slice(p * part, (p + 1) * part)
        left = jnp.concatenate([plain[:, cut], turned[:, cut]], axis=1)
        branch_high, branch_low = split_pair(held[p].reshape(2 * part, columns))
        both = both + dot(left, branch_high)
        low = low + dot(left[: 2 * rows], branch_low)
    sums = both[: 2 * rows] + both[2 * rows :] + low
    for tile in range(columns // LANES):
        lanes = slice(tile * LANES, (tile + 1) * LANES)
        pack(chunks, tile, width, sums[:rows, lanes], sums[rows:, lanes])
    exchange_ready(out_refs, chunks, axis)


def relabel(step, order_ref, from_ref, to_ref, copies):
    columns = to_ref.shape[1]
    part = columns // len(copies)
    meets = one_hot(order_ref, step, columns)
    for h, copy in enumerate(copies):
        if copy is not None:
            copy.wait()
        cut = slice(h * part, (h + 1) * part)
        for c in range(2):
            high, low = split_pair(from_ref[c, :, cut])
            to_ref[c, :, cut] = dot(meets, high).astype(jnp.bfloat16)
            to_ref[2 + c, :, cut] = dot(meets, low).astype(jnp.bfloat16)


def second_branch_kernel(order_hbm, after_ref, branches_hbm, to_ref, next_ref, order_ref, held, sems):
    columns = to_ref.shape[1]
    part = columns // HALVES
    order_copy = pltpu.make_async_copy(order_hbm, order_ref, sems.at[0])
    order_copy.start()
    copies = [
        pltpu.make_async_copy(
            branches_hbm.at[1, :, :, pl.ds(h * part, part)], held.at[:, :, pl.ds(h * part, part)], sems.at[2 + h]
        )
        for h in range(HALVES)
    ]
    for copy in copies:
        copy.start()
    next_copy = pltpu.make_async_copy(branches_hbm.at[2], next_ref, sems.at[1])
    next_copy.start()
    order_copy.wait()
    relabel(1, order_ref, held, to_ref, copies)
    next_copy.wait()


def third_branch_kernel(order_hbm, after_ref, from_ref, to_ref, order_ref, sems):
    order_copy = pltpu.make_async_copy(order_hbm, order_ref, sems.at[0])
    order_copy.start()
    order_copy.wait()
    relabel(2, order_ref, from_ref, to_ref, [None] * HALVES)


def received(in_refs, group, axis, chunks, columns):
    if axis is None:
        chunks[...] = in_refs[0][...]
        first = 0
    else:
        size = chunks.shape[0]
        me = lax.axis_index(axis)
        for s, ref in zip(group, in_refs):
            chunks[jnp.bitwise_and(jnp.bitwise_xor(me, s), size - 1)] = ref[...]
        half = jnp.bitwise_xor(me, group[0]) // size
        first = pl.multiple_of(half * columns, columns)
    real, imag = unpack(chunks, columns)
    real_high, real_low = split_pair(real)
    imag_high, imag_low = split_pair(imag)
    return *operands((real_high, imag_high, real_low, imag_low)), first


def early_kernel(group, axis, branch_ref, *refs):
    in_refs, (out_ref, chunks) = refs[:-2], refs[-2:]
    columns = branch_ref.shape[1] // 2
    plain, turned, first = received(in_refs, group, axis, chunks, columns)
    out_ref[...] = contract(plain, turned, [branch_ref[q, pl.ds(first, columns), :] for q in range(4)])


def late_sums(group, axis, sums_ref, branch_ref, in_refs, chunks):
    columns = branch_ref.shape[2] if sums_ref is None else branch_ref.shape[1] // 2
    plain, turned, first = received(in_refs, group, axis, chunks, columns)
    part = branch_ref.shape[2] // HALVES
    for h in range(HALVES):
        cut = slice(h * part, (h + 1) * part)
        sums = contract(plain, turned, [branch_ref[q, pl.ds(first, columns), cut] for q in range(4)])
        yield h * part, sums if sums_ref is None else sums + sums_ref[:, cut]


def middle_kernel(group, early, in_axis, out_axis, *refs):
    sums_ref, refs = (refs[0], refs[1:]) if early else (None, refs)
    branch_ref, *refs = refs
    in_refs, out_refs, (arrived, chunks) = refs[: len(group)], refs[len(group) : -2], refs[-2:]
    width = branch_ref.shape[2] // chunks.shape[0]
    for start, sums in late_sums(group, in_axis, sums_ref, branch_ref, in_refs, arrived):
        rows = sums.shape[0] // 2
        for tile in range(sums.shape[1] // LANES):
            lanes = slice(tile * LANES, (tile + 1) * LANES)
            pack(chunks, start // LANES + tile, width, sums[:rows, lanes], sums[rows:, lanes])
    exchange_ready(out_refs, chunks, out_axis)


def last_kernel(group, early, in_axis, *refs):
    sums_ref, refs = (refs[0], refs[1:]) if early else (None, refs)
    branch_ref, *refs = refs
    in_refs, (out_hbm, arrived, done, sems) = refs[: len(group)], refs[len(group) :]
    copies = []
    for h, (start, sums) in enumerate(late_sums(group, in_axis, sums_ref, branch_ref, in_refs, arrived)):
        rows = sums.shape[0] // 2
        done[h, 0] = sums[:rows].T
        done[h, 1] = sums[rows:].T
        copy = pltpu.make_async_copy(done.at[h], out_hbm.at[:, pl.ds(start, sums.shape[1]), :], sems.at[h])
        copy.start()
        copies.append(copy)
    for copy in copies:
        copy.wait()


def swap(outs, axis):
    size = lax.axis_size(axis)
    if size > DIRECT:
        return [lax.all_to_all(outs[0], axis, split_axis=0, concat_axis=0, tiled=True)]
    order = partners(size)
    return list(outs[:1]) + [
        lax.ppermute(out, axis, [(i, i ^ s) for i in range(size)]) for s, out in zip(order[1:], outs[1:])
    ]


HBM = pl.BlockSpec(memory_space=pltpu.HBM)
VMEM = pl.BlockSpec(memory_space=pltpu.VMEM)
ANY = pl.BlockSpec(memory_space=pl.ANY)


def call(kernel, out_shape, in_specs, out_specs, scratch, flops, args):
    params = pltpu.CompilerParams(vmem_limit_bytes=VMEM_LIMIT)
    cost = pl.CostEstimate(flops=flops, bytes_accessed=4 << 20, transcendentals=0)
    return pl.pallas_call(
        kernel, out_shape=out_shape, in_specs=in_specs, out_specs=out_specs, scratch_shapes=scratch,
        compiler_params=params, cost_estimate=cost,
    )(*args)


def body(stem, branches, mode_order):
    columns, rows = stem.shape[3:]
    part = columns // HALVES

    def block(axis):
        size = lax.axis_size(axis)
        return size, rows * columns // size // LANES + SUBLANES, LANES

    def coded(axis):
        shape = block(axis)
        if shape[0] > DIRECT:
            return [jax.ShapeDtypeStruct(shape, jnp.int32)]
        return [jax.ShapeDtypeStruct(shape[1:], jnp.int32)] * shape[0]

    def arrays(axis):
        return pltpu.VMEM(block(axis), jnp.int32)

    branches = pltpu.with_memory_space_constraint(branches, pltpu.HBM)
    mode_order = pltpu.with_memory_space_constraint(mode_order, pltpu.HBM)
    local = pltpu.with_memory_space_constraint(stem.reshape(2, columns, rows), pltpu.HBM)
    order = pltpu.SMEM(mode_order.shape, jnp.int32)
    product = 24 * rows * columns * columns

    ready = jax.ShapeDtypeStruct((4, columns, columns), jnp.bfloat16)
    partial = jax.ShapeDtypeStruct((2 * rows, columns), jnp.float32)

    def contracted(kernel, axis, branch, outs, early, out_shape, out_specs, scratch):
        size, height, _ = block(axis)
        if size > DIRECT:
            return call(
                functools.partial(kernel, (0,), False, None), out_shape, [VMEM] * 2, out_specs,
                [arrays(axis), *scratch], product, (branch, *outs))
        order = partners(size)
        arrived = pltpu.VMEM((size // 2, height, LANES), jnp.int32)
        late = [s for s in order if s not in early]
        first = call(
            functools.partial(early_kernel, early, axis), partial, [VMEM] * (1 + len(early)), VMEM, [arrived],
            product // 2, (branch, *(outs[order.index(s)] for s in early)))
        return call(
            functools.partial(kernel, late, True, axis), out_shape, [VMEM] * (2 + len(late)), out_specs,
            [arrived, *scratch], product // 2, (first, branch, *(outs[order.index(s)] for s in late)))

    shapes = coded("narrow")
    outs = call(
        functools.partial(first_kernel, "narrow"), shapes, [HBM] * 3, [VMEM] * len(shapes),
        [order, pltpu.VMEM(local.shape, jnp.float32), pltpu.VMEM((PARTS, 2, columns // PARTS, columns), jnp.float32),
         arrays("narrow"), pltpu.SemaphoreType.DMA((2 + PARTS,))],
        product, (mode_order, local, branches))
    whole_branch = jax.ShapeDtypeStruct(branches.shape[1:], jnp.float32)
    second_branch, third_branch = call(
        second_branch_kernel, [ready, whole_branch], [HBM, ANY, HBM], [VMEM, VMEM],
        [order, pltpu.VMEM(branches.shape[1:], jnp.float32), pltpu.SemaphoreType.DMA((2 + HALVES,))],
        8 * columns**3, (mode_order, outs[0], branches))
    outs = swap(outs, "narrow")
    size = lax.axis_size("narrow")
    shapes = coded("wide")
    outs = contracted(
        lambda group, early, axis, *refs: middle_kernel(group, early, axis, "wide", *refs),
        "narrow", second_branch, outs, partners_near(size), shapes, [VMEM] * len(shapes), [arrays("wide")])
    (third_branch,) = call(
        third_branch_kernel, [ready], [HBM, ANY, VMEM], [VMEM], [order, pltpu.SemaphoreType.DMA((1,))],
        8 * columns**3, (mode_order, outs[0], third_branch))
    outs = swap(outs, "wide")
    size = lax.axis_size("wide")
    final = contracted(
        lambda group, early, axis, *refs: last_kernel(group, early, axis, *refs),
        "wide", third_branch, outs, partners_far(size), jax.ShapeDtypeStruct((2, columns, rows), jnp.float32), HBM,
        [pltpu.VMEM((HALVES, 2, part, rows), jnp.float32), pltpu.SemaphoreType.DMA((HALVES,))])
    return final.reshape(2, 1, 1, columns, rows)


def solution(mesh):
    return jax.shard_map(
        body,
        mesh=mesh,
        in_specs=(P(None, "wide", "narrow", None, None), P(), P()),
        out_specs=P(None, "wide", "narrow", None, None),
        check_vma=False,
    )
```

```python
import functools

import jax
import jax.numpy as jnp
from jax import lax
from jax.experimental import pallas as pl
from jax.experimental.pallas import tpu as pltpu
from jax.sharding import PartitionSpec as P

LANES = 128
SUBLANES = 8
TOP = 32766.0
FINE = 65536.0
HALVES = 2
PARTS = 2
DIRECT = 8
VMEM_LIMIT = 24 << 20


def split_pair(values):
    high = values.astype(jnp.bfloat16)
    low = (values - high.astype(jnp.float32)).astype(jnp.bfloat16)
    return high, low


def dot(left, right):
    return lax.dot_general(left, right, (((1,), (0,)), ((), ())), preferred_element_type=jnp.float32)


def one_hot(order_ref, step, columns):
    row = lax.broadcasted_iota(jnp.int32, (SUBLANES, columns), 1)
    meets = jnp.zeros_like(row)
    for b in range(order_ref.shape[1]):
        bit = jnp.bitwise_and(jnp.right_shift(row, order_ref[step, b]), 1)
        meets = meets + jnp.left_shift(bit, b)
    column = lax.broadcasted_iota(jnp.int32, (columns, columns), 0)
    return jnp.where(column == meets[0:1, :], 1.0, 0.0).astype(jnp.bfloat16)


def operands(pieces):
    real_high, imag_high, real_low, imag_low = pieces
    plain = jnp.concatenate([real_high, imag_high, real_low, imag_low], axis=0)
    turned = jnp.concatenate([-imag_high, real_high, -imag_low, real_low], axis=0)
    return plain, turned


def contract(plain, turned, branch):
    real_high, imag_high, real_low, imag_low = branch
    rows = plain.shape[0] // 2
    both = dot(plain, real_high) + dot(turned, imag_high)
    low = dot(plain[:rows], real_low) + dot(turned[:rows], imag_low)
    return both[:rows] + both[rows:] + low


def lane_block(shape, width):
    return lax.broadcasted_iota(jnp.int32, shape, 1) // width


def rotate(values, amount):
    amount = amount % LANES
    return pltpu.roll(values, amount, 1) if amount else values


def encode(out_ref, slot, real, imag):
    rows = real.shape[0]
    tall = jnp.maximum(jnp.abs(real), jnp.abs(imag)).reshape(rows // SUBLANES, SUBLANES, LANES)
    largest = jnp.maximum(jnp.max(tall, axis=0), 1e-30)
    level = jnp.ceil(jnp.log2(largest) * FINE)
    gain = jnp.exp2(level * (-1.0 / FINE)) * TOP
    gain = jnp.broadcast_to(gain[None], tall.shape).reshape(rows, LANES)
    upper = jnp.round(real * gain).astype(jnp.int32)
    lower = jnp.round(imag * gain).astype(jnp.int32)
    out_ref[slot, 0:rows, :] = jnp.bitwise_or(jnp.left_shift(upper, 16), jnp.bitwise_and(lower, 0xFFFF))
    out_ref[slot, rows : rows + SUBLANES, :] = level.astype(jnp.int32)


def decode(in_ref, slot):
    rows = in_ref.shape[1] - SUBLANES
    codes = in_ref[slot, 0:rows, :]
    level = in_ref[slot, rows : rows + SUBLANES, :].astype(jnp.float32)
    step = jnp.exp2(level * (1.0 / FINE)) * (1.0 / TOP)
    step = jnp.broadcast_to(step[None], (rows // SUBLANES, SUBLANES, LANES)).reshape(rows, LANES)
    real = jnp.right_shift(codes, 16).astype(jnp.float32) * step
    imag = jnp.right_shift(jnp.left_shift(codes, 16), 16).astype(jnp.float32) * step
    return real, imag


def pack(out_ref, tile, width, real, imag):
    share = LANES // width
    height = real.shape[0] // share
    for p in range(share):
        made = []
        for values in (real, imag):
            piece = rotate(values[0:height], -p * width)
            for q in range(1, share):
                other = rotate(values[q * height : (q + 1) * height], (q - p) * width)
                piece = jnp.where(lane_block(other.shape, width) == q, other, piece)
            made.append(piece)
        encode(out_ref, tile * share + p, *made)


def unpack(in_ref, columns):
    blocks = in_ref.shape[0]
    width = columns // blocks
    share = LANES // width
    tiles = []
    for tile in range(columns // LANES):
        got = [decode(in_ref, tile * share + p) for p in range(share)]
        both = []
        for c in range(2):
            groups = []
            for q in range(share):
                piece = rotate(got[0][c], -q * width)
                for p in range(1, share):
                    other = rotate(got[p][c], (p - q) * width)
                    piece = jnp.where(lane_block(other.shape, width) == p, other, piece)
                groups.append(piece)
            both.append(jnp.concatenate(groups, axis=0) if share > 1 else groups[0])
        tiles.append(both)
    return tuple(jnp.concatenate([t[c] for t in tiles], axis=1) for c in range(2))


def partners(size):
    half = size // 2
    return [0] + sorted(range(1, size), key=lambda s: (s < half, -(s % 2), -s))


def partners_near(size):
    return [s for s in partners(size) if s < size // 2]


def partners_far(size):
    return [s for s in partners(size) if s >= size // 2]


def exchange_ready(out_refs, chunks, axis):
    if len(out_refs) == 1:
        out_refs[0][...] = chunks[...]
        return
    me = lax.axis_index(axis)
    for s, ref in zip(partners(len(out_refs)), out_refs):
        ref[...] = chunks[jnp.bitwise_xor(me, s)]


def first_kernel(axis, order_hbm, stem_hbm, branches_hbm, *refs):
    *out_refs, order_ref, stem_ref, held, chunks, sems = refs
    parts, _, part, columns = held.shape
    width = columns // chunks.shape[0]
    order_copy = pltpu.make_async_copy(order_hbm, order_ref, sems.at[0])
    stem_copies = [pltpu.make_async_copy(stem_hbm.at[c], stem_ref.at[c], sems.at[1 + c]) for c in range(2)]
    copies = [
        pltpu.make_async_copy(branches_hbm.at[0, :, pl.ds(p * part, part), :], held.at[p], sems.at[3 + p])
        for p in range(parts)
    ]
    for copy in [order_copy, *stem_copies, *copies]:
        copy.start()
    order_copy.wait()
    meets = one_hot(order_ref, 0, columns)
    for copy in stem_copies:
        copy.wait()
    real_high, real_low = split_pair(stem_ref[0].T)
    imag_high, imag_low = split_pair(stem_ref[1].T)
    rows = real_high.shape[0]
    moved = dot(jnp.concatenate([real_high, imag_high, real_low, imag_low], axis=0), meets).astype(jnp.bfloat16)
    plain, turned = operands([moved[q * rows : (q + 1) * rows] for q in range(4)])
    sums = None
    for p, copy in enumerate(copies):
        copy.wait()
        cut = slice(p * part, (p + 1) * part)
        real_high, real_low = split_pair(held[p, 0])
        imag_high, imag_low = split_pair(held[p, 1])
        more = contract(plain[:, cut], turned[:, cut], (real_high, imag_high, real_low, imag_low))
        sums = more if sums is None else sums + more
    for tile in range(columns // LANES):
        lanes = slice(tile * LANES, (tile + 1) * LANES)
        pack(chunks, tile, width, sums[:rows, lanes], sums[rows:, lanes])
    exchange_ready(out_refs, chunks, axis)


def relabel(meets, from_ref, to_ref):
    for c in range(2):
        high, low = split_pair(from_ref[c])
        to_ref[c] = dot(meets, high).astype(jnp.bfloat16)
        to_ref[2 + c] = dot(meets, low).astype(jnp.bfloat16)


def branches_kernel(order_hbm, after_ref, branches_hbm, *refs):
    second_refs, (third_ref, rest_ref, meets_ref, order_ref, held, sems) = refs[:HALVES], refs[HALVES:]
    columns, part = held.shape[2:]
    order_copy = pltpu.make_async_copy(order_hbm, order_ref, sems.at[0])
    order_copy.start()
    copies = []
    for h in range(HALVES + 2):
        step, at = 1 + h // HALVES, h % HALVES
        to = held.at[h] if h <= HALVES else rest_ref
        copy = pltpu.make_async_copy(branches_hbm.at[step, :, :, pl.ds(at * part, part)], to, sems.at[1 + h])
        copy.start()
        copies.append(copy)
    order_copy.wait()
    meets = one_hot(order_ref, 1, columns)
    meets_ref[...] = one_hot(order_ref, 2, columns)
    for h in range(HALVES):
        copies[h].wait()
        relabel(meets, held.at[h], second_refs[h])
    copies[HALVES].wait()
    relabel(meets_ref[...], held.at[HALVES], third_ref)
    copies[HALVES + 1].wait()


def rest_kernel(after_ref, meets_ref, from_ref, to_ref):
    relabel(meets_ref[...], from_ref, to_ref)


def received(in_refs, group, axis, chunks, columns):
    if axis is None:
        chunks[...] = in_refs[0][...]
        first = 0
    else:
        size = chunks.shape[0]
        me = lax.axis_index(axis)
        for s, ref in zip(group, in_refs):
            chunks[jnp.bitwise_and(jnp.bitwise_xor(me, s), size - 1)] = ref[...]
        half = jnp.bitwise_xor(me, group[0]) // size
        first = pl.multiple_of(half * columns, columns)
    real, imag = unpack(chunks, columns)
    real_high, real_low = split_pair(real)
    imag_high, imag_low = split_pair(imag)
    return *operands((real_high, imag_high, real_low, imag_low)), first


def early_kernel(group, axis, *refs):
    branch_refs, in_refs, (out_ref, chunks) = refs[:HALVES], refs[HALVES:-2], refs[-2:]
    columns = branch_refs[0].shape[1] // 2
    plain, turned, first = received(in_refs, group, axis, chunks, columns)
    part = branch_refs[0].shape[2]
    for h, ref in enumerate(branch_refs):
        out_ref[:, h * part : (h + 1) * part] = contract(
            plain, turned, [ref[q, pl.ds(first, columns), :] for q in range(4)]
        )


def late_sums(group, early, axis, refs, chunks):
    sums_ref, refs = (refs[0], refs[1:]) if early else (None, refs)
    branch_refs, in_refs = refs[:HALVES], refs[HALVES:]
    columns = branch_refs[0].shape[1] // (2 if early else 1)
    plain, turned, first = received(in_refs, group, axis, chunks, columns)
    part = branch_refs[0].shape[2]
    for h, ref in enumerate(branch_refs):
        sums = contract(plain, turned, [ref[q, pl.ds(first, columns), :] for q in range(4)])
        yield h, part, sums + sums_ref[:, h * part : (h + 1) * part] if early else sums


def middle_kernel(group, early, in_axis, out_axis, *refs):
    ins = early + HALVES + len(group)
    out_refs, (arrived, chunks) = refs[ins:-2], refs[-2:]
    for h, part, sums in late_sums(group, early, in_axis, refs[:ins], arrived):
        rows = sums.shape[0] // 2
        width = part * HALVES // chunks.shape[0]
        for tile in range(part // LANES):
            lanes = slice(tile * LANES, (tile + 1) * LANES)
            pack(chunks, h * (part // LANES) + tile, width, sums[:rows, lanes], sums[rows:, lanes])
    exchange_ready(out_refs, chunks, out_axis)


def last_kernel(group, early, in_axis, *refs):
    ins = early + HALVES + len(group)
    out_hbm, arrived, done, sems = refs[ins:]
    copies = []
    for h, part, sums in late_sums(group, early, in_axis, refs[:ins], arrived):
        rows = sums.shape[0] // 2
        for c in range(2):
            done[h, c] = sums[c * rows : (c + 1) * rows].T
            copy = pltpu.make_async_copy(done.at[h, c], out_hbm.at[c, pl.ds(h * part, part), :], sems.at[2 * h + c])
            copy.start()
            copies.append(copy)
    for copy in copies:
        copy.wait()


def swap(outs, axis):
    size = lax.axis_size(axis)
    if size > DIRECT:
        return [lax.all_to_all(outs[0], axis, split_axis=0, concat_axis=0, tiled=True)]
    order = partners(size)
    return list(outs[:1]) + [
        lax.ppermute(out, axis, [(i, i ^ s) for i in range(size)]) for s, out in zip(order[1:], outs[1:])
    ]


HBM = pl.BlockSpec(memory_space=pltpu.HBM)
VMEM = pl.BlockSpec(memory_space=pltpu.VMEM)
ANY = pl.BlockSpec(memory_space=pl.ANY)


def call(kernel, out_shape, in_specs, out_specs, scratch, flops, args):
    params = pltpu.CompilerParams(vmem_limit_bytes=VMEM_LIMIT)
    cost = pl.CostEstimate(flops=flops, bytes_accessed=4 << 20, transcendentals=0)
    return pl.pallas_call(
        kernel, out_shape=out_shape, in_specs=in_specs, out_specs=out_specs, scratch_shapes=scratch,
        compiler_params=params, cost_estimate=cost,
    )(*args)


def body(stem, branches, mode_order):
    columns, rows = stem.shape[3:]
    part = columns // HALVES

    def block(axis):
        size = lax.axis_size(axis)
        return size, rows * columns // size // LANES + SUBLANES, LANES

    def coded(axis):
        shape = block(axis)
        if shape[0] > DIRECT:
            return [jax.ShapeDtypeStruct(shape, jnp.int32)]
        return [jax.ShapeDtypeStruct(shape[1:], jnp.int32)] * shape[0]

    def arrays(axis):
        return pltpu.VMEM(block(axis), jnp.int32)

    branches = pltpu.with_memory_space_constraint(branches, pltpu.HBM)
    mode_order = pltpu.with_memory_space_constraint(mode_order, pltpu.HBM)
    local = pltpu.with_memory_space_constraint(stem.reshape(2, columns, rows), pltpu.HBM)
    order = pltpu.SMEM(mode_order.shape, jnp.int32)
    product = 24 * rows * columns * columns

    ready = jax.ShapeDtypeStruct((4, columns, part), jnp.bfloat16)
    partial = jax.ShapeDtypeStruct((2 * rows, columns), jnp.float32)

    def contracted(kernel, axis, branch, outs, early, out_shape, out_specs, scratch):
        size, height, _ = block(axis)
        if size > DIRECT:
            return call(
                functools.partial(kernel, (0,), 0, None), out_shape, [VMEM] * (HALVES + 1), out_specs,
                [arrays(axis), *scratch], product, (*branch, *outs))
        order = partners(size)
        arrived = pltpu.VMEM((size // 2, height, LANES), jnp.int32)
        late = [s for s in order if s not in early]
        first = call(
            functools.partial(early_kernel, early, axis), partial, [VMEM] * (HALVES + len(early)), VMEM, [arrived],
            product // 2, (*branch, *(outs[order.index(s)] for s in early)))
        return call(
            functools.partial(kernel, late, 1, axis), out_shape, [VMEM] * (1 + HALVES + len(late)), out_specs,
            [arrived, *scratch], product // 2, (first, *branch, *(outs[order.index(s)] for s in late)))

    shapes = coded("narrow")
    outs = call(
        functools.partial(first_kernel, "narrow"), shapes, [HBM] * 3, [VMEM] * len(shapes),
        [order, pltpu.VMEM(local.shape, jnp.float32), pltpu.VMEM((PARTS, 2, columns // PARTS, columns), jnp.float32),
         arrays("narrow"), pltpu.SemaphoreType.DMA((3 + PARTS,))],
        product, (mode_order, local, branches))
    half_branch = (2, columns, part)
    *second_branch, third_half, rest, meets = call(
        branches_kernel,
        [ready] * HALVES
        + [ready, jax.ShapeDtypeStruct(half_branch, jnp.float32), jax.ShapeDtypeStruct((columns, columns), jnp.bfloat16)],
        [HBM, ANY, HBM], [VMEM] * (HALVES + 3),
        [order, pltpu.VMEM((HALVES + 1, *half_branch), jnp.float32), pltpu.SemaphoreType.DMA((HALVES + 3,))],
        12 * columns**3, (mode_order, outs[0], branches))
    outs = swap(outs, "narrow")
    size = lax.axis_size("narrow")
    shapes = coded("wide")
    outs = contracted(
        lambda group, early, axis, *refs: middle_kernel(group, early, axis, "wide", *refs),
        "narrow", second_branch, outs, partners_near(size), shapes, [VMEM] * len(shapes), [arrays("wide")])
    other_half = call(rest_kernel, ready, [ANY, VMEM, VMEM], VMEM, [], 4 * columns**3, (outs[0], meets, rest))
    outs = swap(outs, "wide")
    size = lax.axis_size("wide")
    final = contracted(
        last_kernel, "wide", (third_half, other_half), outs, partners_far(size),
        jax.ShapeDtypeStruct((2, columns, rows), jnp.float32), HBM,
        [pltpu.VMEM((HALVES, 2, part, rows), jnp.float32), pltpu.SemaphoreType.DMA((2 * HALVES,))])
    return final.reshape(2, 1, 1, columns, rows)


def solution(mesh):
    return jax.shard_map(
        body,
        mesh=mesh,
        in_specs=(P(None, "wide", "narrow", None, None), P(), P()),
        out_specs=P(None, "wide", "narrow", None, None),
        check_vma=False,
    )
```

```python
import functools

import jax
import jax.numpy as jnp
from jax import lax
from jax.experimental import pallas as pl
from jax.experimental.pallas import tpu as pltpu
from jax.sharding import PartitionSpec as P

LANES = 128
SUBLANES = 8
TOP = 32766.0
FINE = 65536.0
HALVES = 2
DIRECT = 8
VMEM_LIMIT = 24 << 20


def split_pair(values):
    high = values.astype(jnp.bfloat16)
    low = (values - high.astype(jnp.float32)).astype(jnp.bfloat16)
    return high, low


def dot(left, right):
    return lax.dot_general(left, right, (((1,), (0,)), ((), ())), preferred_element_type=jnp.float32)


def one_hot(order_ref, step, columns):
    row = lax.broadcasted_iota(jnp.int32, (SUBLANES, columns), 1)
    meets = jnp.zeros_like(row)
    for b in range(order_ref.shape[1]):
        bit = jnp.bitwise_and(jnp.right_shift(row, order_ref[step, b]), 1)
        meets = meets + jnp.left_shift(bit, b)
    column = lax.broadcasted_iota(jnp.int32, (columns, columns), 0)
    return jnp.where(column == meets[0:1, :], 1.0, 0.0).astype(jnp.bfloat16)


def operands(pieces):
    real_high, imag_high, real_low, imag_low = pieces
    plain = jnp.concatenate([real_high, imag_high, real_low, imag_low], axis=0)
    turned = jnp.concatenate([-imag_high, real_high, -imag_low, real_low], axis=0)
    return plain, turned


def contract(plain, turned, high, low):
    rows = plain.shape[0] // 2
    left = jnp.concatenate([plain, turned], axis=1)
    both = dot(left, high)
    return both[:rows] + both[rows:] + dot(left[:rows], low)


def lane_block(shape, width):
    return lax.broadcasted_iota(jnp.int32, shape, 1) // width


def rotate(values, amount):
    amount = amount % LANES
    return pltpu.roll(values, amount, 1) if amount else values


def encode(out_ref, slot, real, imag):
    rows = real.shape[0]
    tall = jnp.maximum(jnp.abs(real), jnp.abs(imag)).reshape(rows // SUBLANES, SUBLANES, LANES)
    largest = jnp.maximum(jnp.max(tall, axis=0), 1e-30)
    level = jnp.ceil(jnp.log2(largest) * FINE)
    gain = jnp.exp2(level * (-1.0 / FINE)) * TOP
    gain = jnp.broadcast_to(gain[None], tall.shape).reshape(rows, LANES)
    upper = jnp.round(real * gain).astype(jnp.int32)
    lower = jnp.round(imag * gain).astype(jnp.int32)
    out_ref[slot, 0:rows, :] = jnp.bitwise_or(jnp.left_shift(upper, 16), jnp.bitwise_and(lower, 0xFFFF))
    out_ref[slot, rows : rows + SUBLANES, :] = level.astype(jnp.int32)


def decode(in_ref, slot):
    rows = in_ref.shape[1] - SUBLANES
    codes = in_ref[slot, 0:rows, :]
    level = in_ref[slot, rows : rows + SUBLANES, :].astype(jnp.float32)
    step = jnp.exp2(level * (1.0 / FINE)) * (1.0 / TOP)
    step = jnp.broadcast_to(step[None], (rows // SUBLANES, SUBLANES, LANES)).reshape(rows, LANES)
    real = jnp.right_shift(codes, 16).astype(jnp.float32) * step
    imag = jnp.right_shift(jnp.left_shift(codes, 16), 16).astype(jnp.float32) * step
    return real, imag


def pack(out_ref, tile, width, real, imag):
    share = LANES // width
    height = real.shape[0] // share
    for p in range(share):
        made = []
        for values in (real, imag):
            piece = rotate(values[0:height], -p * width)
            for q in range(1, share):
                other = rotate(values[q * height : (q + 1) * height], (q - p) * width)
                piece = jnp.where(lane_block(other.shape, width) == q, other, piece)
            made.append(piece)
        encode(out_ref, tile * share + p, *made)


def unpack(in_ref, columns):
    blocks = in_ref.shape[0]
    width = columns // blocks
    share = LANES // width
    tiles = []
    for tile in range(columns // LANES):
        got = [decode(in_ref, tile * share + p) for p in range(share)]
        both = []
        for c in range(2):
            groups = []
            for q in range(share):
                piece = rotate(got[0][c], -q * width)
                for p in range(1, share):
                    other = rotate(got[p][c], (p - q) * width)
                    piece = jnp.where(lane_block(other.shape, width) == p, other, piece)
                groups.append(piece)
            both.append(jnp.concatenate(groups, axis=0) if share > 1 else groups[0])
        tiles.append(both)
    return tuple(jnp.concatenate([t[c] for t in tiles], axis=1) for c in range(2))


def partners(size):
    half = size // 2
    far = sorted(range(half, size), key=lambda s: (-(s % 2), -s))
    near = sorted(range(1, half), key=lambda s: (s > 1, -s))
    return [0, *far, *near]


def last_group(size):
    half = size // 2

    def run(first, end):
        return [s for s in partners(size) if first <= s < end]

    if half <= 2:
        return run(half, size), [run(0, half)]
    return run(half // 2, half), [run(half, size), run(0, half // 2)]


def exchange_ready(out_refs, chunks, axis):
    if len(out_refs) == 1:
        out_refs[0][...] = chunks[...]
        return
    me = lax.axis_index(axis)
    for s, ref in zip(partners(len(out_refs)), out_refs):
        ref[...] = chunks[jnp.bitwise_xor(me, s)]


def copies_of_stem(order_hbm, stem_hbm, order_ref, stem_ref, sems):
    copies = [pltpu.make_async_copy(order_hbm, order_ref, sems.at[0])]
    copies += [pltpu.make_async_copy(stem_hbm.at[c], stem_ref.at[c], sems.at[1 + c]) for c in range(2)]
    for copy in copies:
        copy.start()
    return copies


def relabelled_stem(order_ref, stem_ref, copies):
    copies[0].wait()
    meets = one_hot(order_ref, 0, stem_ref.shape[1])
    for copy in copies[1:]:
        copy.wait()
    real_high, real_low = split_pair(stem_ref[0].T)
    imag_high, imag_low = split_pair(stem_ref[1].T)
    return dot(jnp.concatenate([real_high, imag_high, real_low, imag_low], axis=0), meets).astype(jnp.bfloat16)


def four(pieces):
    rows = pieces.shape[0] // 4
    return operands([pieces[q * rows : (q + 1) * rows] for q in range(4)])


def pack_all(chunks, first, width, sums):
    rows = sums.shape[0] // 2
    for tile in range(sums.shape[1] // LANES):
        lanes = slice(tile * LANES, (tile + 1) * LANES)
        pack(chunks, first + tile, width, sums[:rows, lanes], sums[rows:, lanes])


def whole_kernel(axis, order_hbm, stem_hbm, branches_hbm, out_ref, order_ref, stem_ref, held, chunks, sems):
    columns = held.shape[1]
    copies = copies_of_stem(order_hbm, stem_hbm, order_ref, stem_ref, sems)
    copy = pltpu.make_async_copy(branches_hbm.at[0], held, sems.at[3])
    copy.start()
    plain, turned = four(relabelled_stem(order_ref, stem_ref, copies))
    copy.wait()
    high, low = split_pair(held[...].reshape(2 * columns, columns))
    pack_all(chunks, 0, columns // chunks.shape[0], contract(plain, turned, high, low))
    exchange_ready((out_ref,), chunks, axis)


def far_kernel(axis, order_hbm, stem_hbm, branches_hbm, *refs):
    *out_refs, moved_ref, near_ref, order_ref, stem_ref, held, chunks, sems = refs
    columns, part = held.shape[1:]
    size = 2 * len(out_refs)
    me = lax.axis_index(axis)
    near = pl.multiple_of(me // (size // 2) * part, part)
    far = pl.multiple_of((1 - me // (size // 2)) * part, part)
    copies = copies_of_stem(order_hbm, stem_hbm, order_ref, stem_ref, sems)
    copy = pltpu.make_async_copy(branches_hbm.at[0, :, :, pl.ds(far, part)], held, sems.at[3])
    near_copy = pltpu.make_async_copy(branches_hbm.at[0, :, :, pl.ds(near, part)], near_ref, sems.at[4])
    copy.start()
    near_copy.start()
    moved = relabelled_stem(order_ref, stem_ref, copies)
    moved_ref[...] = moved
    plain, turned = four(moved)
    copy.wait()
    high, low = split_pair(held[...].reshape(2 * columns, part))
    pack_all(chunks, 0, columns // size, contract(plain, turned, high, low))
    for s, ref in zip([s for s in partners(size) if s >= size // 2], out_refs):
        ref[...] = chunks[jnp.bitwise_and(jnp.bitwise_xor(me, s), size // 2 - 1)]
    near_copy.wait()


def near_kernel(axis, order_hbm, moved_ref, near_ref, branches_hbm, *refs):
    *out_refs, next_ref, second_meets, third_meets, order_ref, chunks, sems = refs
    columns, part = near_ref.shape[1:]
    size = 2 * len(out_refs)
    me = lax.axis_index(axis)
    order_copy = pltpu.make_async_copy(order_hbm, order_ref, sems.at[0])
    next_copy = pltpu.make_async_copy(branches_hbm.at[1], next_ref, sems.at[1])
    order_copy.start()
    next_copy.start()
    plain, turned = four(moved_ref[...])
    high, low = split_pair(near_ref[...].reshape(2 * columns, part))
    pack_all(chunks, 0, columns // size, contract(plain, turned, high, low))
    for s, ref in zip([s for s in partners(size) if s < size // 2], out_refs):
        ref[...] = chunks[jnp.bitwise_and(jnp.bitwise_xor(me, s), size // 2 - 1)]
    order_copy.wait()
    second_meets[...] = one_hot(order_ref, 1, columns)
    third_meets[...] = one_hot(order_ref, 2, columns)
    next_copy.wait()


def meets_kernel(order_hbm, after_ref, branches_hbm, next_ref, second_meets, third_meets, order_ref, sems):
    order_copy = pltpu.make_async_copy(order_hbm, order_ref, sems.at[0])
    next_copy = pltpu.make_async_copy(branches_hbm.at[1], next_ref, sems.at[1])
    order_copy.start()
    next_copy.start()
    order_copy.wait()
    second_meets[...] = one_hot(order_ref, 1, next_ref.shape[1])
    third_meets[...] = one_hot(order_ref, 2, next_ref.shape[1])
    next_copy.wait()


def relabel(meets_ref, from_ref, to_refs):
    part = to_refs[0].shape[2]
    for h, to_ref in enumerate(to_refs):
        for c in range(2):
            high, low = split_pair(from_ref[c, :, h * part : (h + 1) * part])
            to_ref[c] = dot(meets_ref[...], high).astype(jnp.bfloat16)
            to_ref[2 + c] = dot(meets_ref[...], low).astype(jnp.bfloat16)


def second_branch_kernel(meets_ref, from_ref, branches_hbm, *refs):
    *to_refs, next_ref, sem = refs
    copy = pltpu.make_async_copy(branches_hbm.at[2], next_ref, sem)
    copy.start()
    relabel(meets_ref, from_ref, to_refs)
    copy.wait()


def third_branch_kernel(after_ref, meets_ref, from_ref, *to_refs):
    relabel(meets_ref, from_ref, to_refs)


def received(in_refs, group, axis, chunks, columns):
    size = len(group)
    if axis is None:
        first = 0
        chunks[...] = in_refs[0][...]
    else:
        me = lax.axis_index(axis)
        for s, ref in zip(group, in_refs):
            chunks[jnp.bitwise_and(jnp.bitwise_xor(me, s), size - 1)] = ref[...]
        first = pl.multiple_of(jnp.bitwise_xor(me, group[0]) // size * columns, columns)
    real, imag = unpack(chunks if axis is None else chunks.at[0:size], columns)
    real_high, real_low = split_pair(real)
    imag_high, imag_low = split_pair(imag)
    return *operands((real_high, imag_high, real_low, imag_low)), first


def rows_of(branch_ref, first, columns):
    part = branch_ref.shape[2]
    high = branch_ref[0:2, pl.ds(first, columns), :].reshape(2 * columns, part)
    low = branch_ref[2:4, pl.ds(first, columns), :].reshape(2 * columns, part)
    return high, low


def early_kernel(groups, axis, *refs):
    branch_refs, in_refs, (out_ref, *chunks) = refs[:HALVES], refs[HALVES : -1 - len(groups)], refs[-1 - len(groups) :]
    size = lax.axis_size(axis)
    part = branch_refs[0].shape[2]
    sums = [None] * HALVES
    for group, held in zip(groups, chunks):
        mine, in_refs = in_refs[: len(group)], in_refs[len(group) :]
        columns = branch_refs[0].shape[1] // size * len(group)
        plain, turned, first = received(mine, group, axis, held, columns)
        for h, ref in enumerate(branch_refs):
            more = contract(plain, turned, *rows_of(ref, first, columns))
            sums[h] = more if sums[h] is None else sums[h] + more
    for h in range(HALVES):
        out_ref[:, h * part : (h + 1) * part] = sums[h]


def late_sums(group, early, axis, refs, chunks):
    sums_ref, refs = (refs[0], refs[1:]) if early else (None, refs)
    branch_refs, in_refs = refs[:HALVES], refs[HALVES:]
    columns = branch_refs[0].shape[1]
    if early:
        columns = columns // lax.axis_size(axis) * len(group)
    plain, turned, first = received(in_refs, group, axis, chunks, columns)
    part = branch_refs[0].shape[2]
    for h, ref in enumerate(branch_refs):
        sums = contract(plain, turned, *rows_of(ref, first, columns))
        yield h, part, sums + sums_ref[:, h * part : (h + 1) * part] if early else sums


def middle_kernel(group, early, in_axis, out_axis, *refs):
    ins = early + HALVES + len(group)
    out_refs, (arrived, chunks) = refs[ins:-2], refs[-2:]
    for h, part, sums in late_sums(group, early, in_axis, refs[:ins], arrived):
        pack_all(chunks, h * (part // LANES), part * HALVES // chunks.shape[0], sums)
    exchange_ready(out_refs, chunks, out_axis)


def last_kernel(group, early, in_axis, *refs):
    ins = early + HALVES + len(group)
    out_hbm, arrived, done, sems = refs[ins:]
    copies = []
    for h, part, sums in late_sums(group, early, in_axis, refs[:ins], arrived):
        rows = sums.shape[0] // 2
        for c in range(2):
            done[h, c] = sums[c * rows : (c + 1) * rows].T
            copy = pltpu.make_async_copy(done.at[h, c], out_hbm.at[c, pl.ds(h * part, part), :], sems.at[2 * h + c])
            copy.start()
            copies.append(copy)
    for copy in copies:
        copy.wait()


def send(out, s, axis):
    return lax.ppermute(out, axis, [(i, i ^ s) for i in range(lax.axis_size(axis))])


def swap(outs, axis):
    size = lax.axis_size(axis)
    if size > DIRECT:
        return {0: lax.all_to_all(outs[0], axis, split_axis=0, concat_axis=0, tiled=True)}
    return {s: out if s == 0 else send(out, s, axis) for s, out in zip(partners(size), outs)}


HBM = pl.BlockSpec(memory_space=pltpu.HBM)
VMEM = pl.BlockSpec(memory_space=pltpu.VMEM)
ANY = pl.BlockSpec(memory_space=pl.ANY)


def call(kernel, out_shape, in_specs, out_specs, scratch, flops, args):
    params = pltpu.CompilerParams(vmem_limit_bytes=VMEM_LIMIT)
    cost = pl.CostEstimate(flops=flops, bytes_accessed=4 << 20, transcendentals=0)
    return pl.pallas_call(
        kernel, out_shape=out_shape, in_specs=in_specs, out_specs=out_specs, scratch_shapes=scratch,
        compiler_params=params, cost_estimate=cost,
    )(*args)


def body(stem, branches, mode_order):
    columns, rows = stem.shape[3:]
    part = columns // HALVES

    def block(axis):
        size = lax.axis_size(axis)
        return size, rows * columns // size // LANES + SUBLANES, LANES

    def coded(axis):
        shape = block(axis)
        if shape[0] > DIRECT:
            return [jax.ShapeDtypeStruct(shape, jnp.int32)]
        return [jax.ShapeDtypeStruct(shape[1:], jnp.int32)] * shape[0]

    def arrays(axis):
        return pltpu.VMEM(block(axis), jnp.int32)

    branches = pltpu.with_memory_space_constraint(branches, pltpu.HBM)
    mode_order = pltpu.with_memory_space_constraint(mode_order, pltpu.HBM)
    local = pltpu.with_memory_space_constraint(stem.reshape(2, columns, rows), pltpu.HBM)
    order = pltpu.SMEM(mode_order.shape, jnp.int32)
    product = 24 * rows * columns * columns

    ready = jax.ShapeDtypeStruct((4, columns, part), jnp.bfloat16)
    partial = jax.ShapeDtypeStruct((2 * rows, columns), jnp.float32)

    def contracted(kernel, axis, branch, got, out_shape, out_specs, scratch):
        size, height, _ = block(axis)
        if size > DIRECT:
            return call(
                functools.partial(kernel, (0,), 0, None), out_shape, [VMEM] * (HALVES + 1), out_specs,
                [arrays(axis), *scratch], product, (*branch, got[0]))

        def held(group):
            return pltpu.VMEM((len(group), height, LANES), jnp.int32)

        last, groups = last_group(size)
        early = [s for group in groups for s in group]
        first = call(
            functools.partial(early_kernel, groups, axis), partial, [VMEM] * (HALVES + len(early)), VMEM,
            [held(group) for group in groups], product // 2, (*branch, *(got[s] for s in early)))
        return call(
            functools.partial(kernel, last, 1, axis), out_shape, [VMEM] * (1 + HALVES + len(last)), out_specs,
            [held(last), *scratch], product // 2, (first, *branch, *(got[s] for s in last)))

    size = lax.axis_size("narrow")
    shapes = coded("narrow")
    whole = jax.ShapeDtypeStruct(branches.shape[1:], jnp.float32)
    meets = jax.ShapeDtypeStruct((columns, columns), jnp.bfloat16)
    stem_scratch = [order, pltpu.VMEM(local.shape, jnp.float32)]
    if size > DIRECT:
        (out,) = call(
            functools.partial(whole_kernel, "narrow"), shapes, [HBM] * 3, [VMEM],
            [*stem_scratch, pltpu.VMEM(whole.shape, jnp.float32), arrays("narrow"), pltpu.SemaphoreType.DMA((4,))],
            product, (mode_order, local, branches))
        got = swap([out], "narrow")
        second_raw, second_meets, third_meets = call(
            meets_kernel, [whole, meets, meets], [HBM, ANY, HBM], [VMEM] * 3,
            [order, pltpu.SemaphoreType.DMA((2,))], columns**2, (mode_order, out, branches))
    else:
        half_blocks = pltpu.VMEM((size // 2, *block("narrow")[1:]), jnp.int32)
        *outs, moved, near = call(
            functools.partial(far_kernel, "narrow"),
            shapes[: size // 2]
            + [jax.ShapeDtypeStruct((4 * rows, columns), jnp.bfloat16), jax.ShapeDtypeStruct((2, columns, part), jnp.float32)],
            [HBM] * 3, [VMEM] * (size // 2 + 2),
            [*stem_scratch, pltpu.VMEM((2, columns, part), jnp.float32), half_blocks, pltpu.SemaphoreType.DMA((5,))],
            product // 2, (mode_order, local, branches))
        order_of = partners(size)
        got = {s: send(out, s, "narrow") for s, out in zip([s for s in order_of if s >= size // 2], outs)}
        *outs, second_raw, second_meets, third_meets = call(
            functools.partial(near_kernel, "narrow"), shapes[: size // 2] + [whole, meets, meets],
            [HBM, VMEM, VMEM, HBM], [VMEM] * (size // 2 + 3),
            [order, half_blocks, pltpu.SemaphoreType.DMA((2,))],
            product // 2, (mode_order, moved, near, branches))
        for s, out in zip([s for s in order_of if s < size // 2], outs):
            got[s] = send(out, s, "narrow") if s else out
    *second_branch, third_raw = call(
        second_branch_kernel, [ready] * HALVES + [whole], [VMEM, VMEM, HBM], [VMEM] * (HALVES + 1),
        [pltpu.SemaphoreType.DMA], 8 * columns**3, (second_meets, second_raw, branches))
    shapes = coded("wide")
    outs = contracted(
        lambda group, early, axis, *refs: middle_kernel(group, early, axis, "wide", *refs),
        "narrow", second_branch, got, shapes, [VMEM] * len(shapes), [arrays("wide")])
    third_branch = call(
        third_branch_kernel, [ready] * HALVES, [ANY, VMEM, VMEM], [VMEM] * HALVES, [], 8 * columns**3,
        (outs[0], third_meets, third_raw))
    got = swap(outs, "wide")
    final = contracted(
        last_kernel, "wide", third_branch, got, jax.ShapeDtypeStruct((2, columns, rows), jnp.float32), HBM,
        [pltpu.VMEM((HALVES, 2, part, rows), jnp.float32), pltpu.SemaphoreType.DMA((2 * HALVES,))])
    return final.reshape(2, 1, 1, columns, rows)


def solution(mesh):
    return jax.shard_map(
        body,
        mesh=mesh,
        in_specs=(P(None, "wide", "narrow", None, None), P(), P()),
        out_specs=P(None, "wide", "narrow", None, None),
        check_vma=False,
    )
```

```python
import functools

import jax
import jax.numpy as jnp
from jax import lax
from jax.experimental import pallas as pl
from jax.experimental.pallas import tpu as pltpu
from jax.sharding import PartitionSpec as P

LANES = 128
SUBLANES = 8
TOP = 32766.0
FINE = 65536.0
HALVES = 2
DIRECT = 8
VMEM_LIMIT = 24 << 20


def split_pair(values):
    high = values.astype(jnp.bfloat16)
    low = (values - high.astype(jnp.float32)).astype(jnp.bfloat16)
    return high, low


def dot(left, right):
    return lax.dot_general(left, right, (((1,), (0,)), ((), ())), preferred_element_type=jnp.float32)


def meets_row(order_ref, step, columns):
    row = lax.broadcasted_iota(jnp.int32, (SUBLANES, columns), 1)
    meets = jnp.zeros_like(row)
    for b in range(order_ref.shape[1]):
        bit = jnp.bitwise_and(jnp.right_shift(row, order_ref[step, b]), 1)
        meets = meets + jnp.left_shift(bit, b)
    return meets


def one_hot(meets):
    columns = meets.shape[1]
    column = lax.broadcasted_iota(jnp.int32, (columns, columns), 0)
    return jnp.where(column == meets[0:1, :], 1.0, 0.0).astype(jnp.bfloat16)


def operands(pieces):
    real_high, imag_high, real_low, imag_low = pieces
    plain = jnp.concatenate([real_high, imag_high, real_low, imag_low], axis=0)
    turned = jnp.concatenate([-imag_high, real_high, -imag_low, real_low], axis=0)
    return plain, turned


def contract(plain, turned, high, low):
    rows = plain.shape[0] // 2
    left = jnp.concatenate([plain, turned], axis=1)
    both = dot(left, high)
    return both[:rows] + both[rows:] + dot(left[:rows], low)


def lane_block(shape, width):
    return lax.broadcasted_iota(jnp.int32, shape, 1) // width


def rotate(values, amount):
    amount = amount % LANES
    return pltpu.roll(values, amount, 1) if amount else values


def encode(out_ref, slot, real, imag):
    rows = real.shape[0]
    tall = jnp.maximum(jnp.abs(real), jnp.abs(imag)).reshape(rows // SUBLANES, SUBLANES, LANES)
    largest = jnp.maximum(jnp.max(tall, axis=0), 1e-30)
    level = jnp.ceil(jnp.log2(largest) * FINE)
    gain = jnp.exp2(level * (-1.0 / FINE)) * TOP
    gain = jnp.broadcast_to(gain[None], tall.shape).reshape(rows, LANES)
    upper = jnp.round(real * gain).astype(jnp.int32)
    lower = jnp.round(imag * gain).astype(jnp.int32)
    out_ref[slot, 0:rows, :] = jnp.bitwise_or(jnp.left_shift(upper, 16), jnp.bitwise_and(lower, 0xFFFF))
    out_ref[slot, rows : rows + SUBLANES, :] = level.astype(jnp.int32)


def decode(in_ref, slot):
    rows = in_ref.shape[1] - SUBLANES
    codes = in_ref[slot, 0:rows, :]
    level = in_ref[slot, rows : rows + SUBLANES, :].astype(jnp.float32)
    step = jnp.exp2(level * (1.0 / FINE)) * (1.0 / TOP)
    step = jnp.broadcast_to(step[None], (rows // SUBLANES, SUBLANES, LANES)).reshape(rows, LANES)
    real = jnp.right_shift(codes, 16).astype(jnp.float32) * step
    imag = jnp.right_shift(jnp.left_shift(codes, 16), 16).astype(jnp.float32) * step
    return real, imag


def pack(out_ref, tile, width, real, imag):
    share = LANES // width
    height = real.shape[0] // share
    for p in range(share):
        made = []
        for values in (real, imag):
            piece = rotate(values[0:height], -p * width)
            for q in range(1, share):
                other = rotate(values[q * height : (q + 1) * height], (q - p) * width)
                piece = jnp.where(lane_block(other.shape, width) == q, other, piece)
            made.append(piece)
        encode(out_ref, tile * share + p, *made)


def unpack(in_ref, columns):
    blocks = in_ref.shape[0]
    width = columns // blocks
    share = LANES // width
    tiles = []
    for tile in range(columns // LANES):
        got = [decode(in_ref, tile * share + p) for p in range(share)]
        both = []
        for c in range(2):
            groups = []
            for q in range(share):
                piece = rotate(got[0][c], -q * width)
                for p in range(1, share):
                    other = rotate(got[p][c], (p - q) * width)
                    piece = jnp.where(lane_block(other.shape, width) == p, other, piece)
                groups.append(piece)
            both.append(jnp.concatenate(groups, axis=0) if share > 1 else groups[0])
        tiles.append(both)
    return tuple(jnp.concatenate([t[c] for t in tiles], axis=1) for c in range(2))


def partners(size):
    half = size // 2
    far = sorted(range(half, size), key=lambda s: (-(s % 2), s if size > 4 else -s))
    near = sorted(range(1, half), key=lambda s: (s > 1, -s))
    return [0, *far, *near]


def last_group(size):
    half = size // 2

    def run(first, end):
        return [s for s in partners(size) if first <= s < end]

    if half <= 2:
        return run(half, size), [run(0, half)]
    return run(half // 2, half), [run(half, size), run(0, half // 2)]


def exchange_ready(out_refs, chunks, axis):
    if len(out_refs) == 1:
        out_refs[0][...] = chunks[...]
        return
    me = lax.axis_index(axis)
    for s, ref in zip(partners(len(out_refs)), out_refs):
        ref[...] = chunks[jnp.bitwise_xor(me, s)]


def copies_of_stem(order_hbm, stem_hbm, order_ref, stem_ref, sems):
    copies = [pltpu.make_async_copy(order_hbm, order_ref, sems.at[0])]
    copies += [pltpu.make_async_copy(stem_hbm.at[c], stem_ref.at[c], sems.at[1 + c]) for c in range(2)]
    for copy in copies:
        copy.start()
    return copies


def relabelled_stem(order_ref, stem_ref, copies):
    copies[0].wait()
    meets = one_hot(meets_row(order_ref, 0, stem_ref.shape[1]))
    for copy in copies[1:]:
        copy.wait()
    rows = stem_ref.shape[2]
    moved = [
        dot(jnp.concatenate(split_pair(stem_ref[c].T), axis=0), meets).astype(jnp.bfloat16) for c in range(2)
    ]
    return jnp.concatenate([moved[0][:rows], moved[1][:rows], moved[0][rows:], moved[1][rows:]], axis=0)


def four(pieces):
    rows = pieces.shape[0] // 4
    return operands([pieces[q * rows : (q + 1) * rows] for q in range(4)])


def pack_all(chunks, first, width, sums):
    rows = sums.shape[0] // 2
    for tile in range(sums.shape[1] // LANES):
        lanes = slice(tile * LANES, (tile + 1) * LANES)
        pack(chunks, first + tile, width, sums[:rows, lanes], sums[rows:, lanes])


def keep_meets(order_ref, meets_ref):
    for step in range(1, order_ref.shape[0]):
        meets_ref[step - 1] = meets_row(order_ref, step, meets_ref.shape[2])


def whole_kernel(axis, order_hbm, stem_hbm, branches_hbm, out_ref, meets_ref, order_ref, stem_ref, held, chunks, sems):
    columns = held.shape[1]
    copies = copies_of_stem(order_hbm, stem_hbm, order_ref, stem_ref, sems)
    copy = pltpu.make_async_copy(branches_hbm.at[0], held, sems.at[3])
    copy.start()
    plain, turned = four(relabelled_stem(order_ref, stem_ref, copies))
    copy.wait()
    high, low = split_pair(held[...].reshape(2 * columns, columns))
    pack_all(chunks, 0, columns // chunks.shape[0], contract(plain, turned, high, low))
    exchange_ready((out_ref,), chunks, axis)
    keep_meets(order_ref, meets_ref)


def far_kernel(axis, order_hbm, stem_hbm, branches_hbm, *refs):
    *out_refs, meets_ref, moved_ref, near_ref, order_ref, stem_ref, held, chunks, sems = refs
    columns, part = held.shape[1:]
    size = 2 * len(out_refs)
    me = lax.axis_index(axis)
    near = pl.multiple_of(me // (size // 2) * part, part)
    far = pl.multiple_of((1 - me // (size // 2)) * part, part)
    copies = copies_of_stem(order_hbm, stem_hbm, order_ref, stem_ref, sems)
    copy = pltpu.make_async_copy(branches_hbm.at[0, :, :, pl.ds(far, part)], held, sems.at[3])
    near_copy = pltpu.make_async_copy(branches_hbm.at[0, :, :, pl.ds(near, part)], near_ref, sems.at[4])
    copy.start()
    near_copy.start()
    moved = relabelled_stem(order_ref, stem_ref, copies)
    moved_ref[...] = moved
    plain, turned = four(moved)
    copy.wait()
    high, low = split_pair(held[...].reshape(2 * columns, part))
    pack_all(chunks, 0, columns // size, contract(plain, turned, high, low))
    for s, ref in zip([s for s in partners(size) if s >= size // 2], out_refs):
        ref[...] = chunks[jnp.bitwise_and(jnp.bitwise_xor(me, s), size // 2 - 1)]
    keep_meets(order_ref, meets_ref)
    near_copy.wait()


def near_kernel(axis, moved_ref, near_ref, meets_ref, branches_hbm, *refs):
    *out_refs, next_ref, second_meets, third_meets, chunks, sem = refs
    columns, part = near_ref.shape[1:]
    size = 2 * len(out_refs)
    me = lax.axis_index(axis)
    next_copy = pltpu.make_async_copy(branches_hbm.at[1], next_ref, sem)
    next_copy.start()
    plain, turned = four(moved_ref[...])
    high, low = split_pair(near_ref[...].reshape(2 * columns, part))
    pack_all(chunks, 0, columns // size, contract(plain, turned, high, low))
    for s, ref in zip([s for s in partners(size) if s < size // 2], out_refs):
        ref[...] = chunks[jnp.bitwise_and(jnp.bitwise_xor(me, s), size // 2 - 1)]
    second_meets[...] = one_hot(meets_ref[0])
    third_meets[...] = one_hot(meets_ref[1])
    next_copy.wait()


def meets_kernel(meets_ref, branches_hbm, next_ref, second_meets, third_meets, sem):
    next_copy = pltpu.make_async_copy(branches_hbm.at[1], next_ref, sem)
    next_copy.start()
    second_meets[...] = one_hot(meets_ref[0])
    third_meets[...] = one_hot(meets_ref[1])
    next_copy.wait()


def relabel(meets_ref, from_ref, to_refs):
    part = to_refs[0].shape[2]
    for h, to_ref in enumerate(to_refs):
        for c in range(2):
            high, low = split_pair(from_ref[c, :, h * part : (h + 1) * part])
            to_ref[c] = dot(meets_ref[...], high).astype(jnp.bfloat16)
            to_ref[2 + c] = dot(meets_ref[...], low).astype(jnp.bfloat16)


def second_branch_kernel(meets_ref, from_ref, branches_hbm, *refs):
    *to_refs, next_ref, sem = refs
    copy = pltpu.make_async_copy(branches_hbm.at[2], next_ref, sem)
    copy.start()
    relabel(meets_ref, from_ref, to_refs)
    copy.wait()


def third_branch_kernel(after_ref, meets_ref, from_ref, *to_refs):
    relabel(meets_ref, from_ref, to_refs)


def received(in_refs, group, axis, chunks, columns):
    size = len(group)
    if axis is None:
        first = 0
        chunks[...] = in_refs[0][...]
    else:
        me = lax.axis_index(axis)
        for s, ref in zip(group, in_refs):
            chunks[jnp.bitwise_and(jnp.bitwise_xor(me, s), size - 1)] = ref[...]
        first = pl.multiple_of(jnp.bitwise_xor(me, group[0]) // size * columns, columns)
    real, imag = unpack(chunks if axis is None else chunks.at[0:size], columns)
    real_high, real_low = split_pair(real)
    imag_high, imag_low = split_pair(imag)
    return *operands((real_high, imag_high, real_low, imag_low)), first


def rows_of(branch_ref, first, columns):
    part = branch_ref.shape[2]
    high = branch_ref[0:2, pl.ds(first, columns), :].reshape(2 * columns, part)
    low = branch_ref[2:4, pl.ds(first, columns), :].reshape(2 * columns, part)
    return high, low


def early_kernel(groups, axis, *refs):
    branch_refs, in_refs, (out_ref, *chunks) = refs[:HALVES], refs[HALVES : -1 - len(groups)], refs[-1 - len(groups) :]
    size = lax.axis_size(axis)
    part = branch_refs[0].shape[2]
    sums = [None] * HALVES
    for group, held in zip(groups, chunks):
        mine, in_refs = in_refs[: len(group)], in_refs[len(group) :]
        columns = branch_refs[0].shape[1] // size * len(group)
        plain, turned, first = received(mine, group, axis, held, columns)
        for h, ref in enumerate(branch_refs):
            more = contract(plain, turned, *rows_of(ref, first, columns))
            sums[h] = more if sums[h] is None else sums[h] + more
    for h in range(HALVES):
        out_ref[:, h * part : (h + 1) * part] = sums[h]


def late_sums(group, early, axis, refs, chunks):
    sums_ref, refs = (refs[0], refs[1:]) if early else (None, refs)
    branch_refs, in_refs = refs[:HALVES], refs[HALVES:]
    columns = branch_refs[0].shape[1]
    if early:
        columns = columns // lax.axis_size(axis) * len(group)
    plain, turned, first = received(in_refs, group, axis, chunks, columns)
    part = branch_refs[0].shape[2]
    for h, ref in enumerate(branch_refs):
        sums = contract(plain, turned, *rows_of(ref, first, columns))
        yield h, part, sums + sums_ref[:, h * part : (h + 1) * part] if early else sums


def middle_kernel(group, early, in_axis, out_axis, *refs):
    ins = early + HALVES + len(group)
    out_refs, (arrived, chunks) = refs[ins:-2], refs[-2:]
    for h, part, sums in late_sums(group, early, in_axis, refs[:ins], arrived):
        pack_all(chunks, h * (part // LANES), part * HALVES // chunks.shape[0], sums)
    exchange_ready(out_refs, chunks, out_axis)


def last_kernel(group, early, in_axis, *refs):
    ins = early + HALVES + len(group)
    out_hbm, arrived, done, sems = refs[ins:]
    copies = []
    for h, part, sums in late_sums(group, early, in_axis, refs[:ins], arrived):
        rows = sums.shape[0] // 2
        for c in range(2):
            done[h, c] = sums[c * rows : (c + 1) * rows].T
            copy = pltpu.make_async_copy(done.at[h, c], out_hbm.at[c, pl.ds(h * part, part), :], sems.at[2 * h + c])
            copy.start()
            copies.append(copy)
    for copy in copies:
        copy.wait()


def send(out, s, axis):
    return lax.ppermute(out, axis, [(i, i ^ s) for i in range(lax.axis_size(axis))])


def swap(outs, axis):
    size = lax.axis_size(axis)
    if size > DIRECT:
        return {0: lax.all_to_all(outs[0], axis, split_axis=0, concat_axis=0, tiled=True)}
    return {s: out if s == 0 else send(out, s, axis) for s, out in zip(partners(size), outs)}


HBM = pl.BlockSpec(memory_space=pltpu.HBM)
VMEM = pl.BlockSpec(memory_space=pltpu.VMEM)
ANY = pl.BlockSpec(memory_space=pl.ANY)


def call(kernel, out_shape, in_specs, out_specs, scratch, flops, args):
    params = pltpu.CompilerParams(vmem_limit_bytes=VMEM_LIMIT)
    cost = pl.CostEstimate(flops=flops, bytes_accessed=4 << 20, transcendentals=0)
    return pl.pallas_call(
        kernel, out_shape=out_shape, in_specs=in_specs, out_specs=out_specs, scratch_shapes=scratch,
        compiler_params=params, cost_estimate=cost,
    )(*args)


def body(stem, branches, mode_order):
    columns, rows = stem.shape[3:]
    part = columns // HALVES

    def block(axis):
        size = lax.axis_size(axis)
        return size, rows * columns // size // LANES + SUBLANES, LANES

    def coded(axis):
        shape = block(axis)
        if shape[0] > DIRECT:
            return [jax.ShapeDtypeStruct(shape, jnp.int32)]
        return [jax.ShapeDtypeStruct(shape[1:], jnp.int32)] * shape[0]

    def arrays(axis):
        return pltpu.VMEM(block(axis), jnp.int32)

    branches = pltpu.with_memory_space_constraint(branches, pltpu.HBM)
    mode_order = pltpu.with_memory_space_constraint(mode_order, pltpu.HBM)
    local = pltpu.with_memory_space_constraint(stem.reshape(2, columns, rows), pltpu.HBM)
    order = pltpu.SMEM(mode_order.shape, jnp.int32)
    product = 24 * rows * columns * columns

    ready = jax.ShapeDtypeStruct((4, columns, part), jnp.bfloat16)
    partial = jax.ShapeDtypeStruct((2 * rows, columns), jnp.float32)

    def contracted(kernel, axis, branch, got, out_shape, out_specs, scratch):
        size, height, _ = block(axis)
        if size > DIRECT:
            return call(
                functools.partial(kernel, (0,), 0, None), out_shape, [VMEM] * (HALVES + 1), out_specs,
                [arrays(axis), *scratch], product, (*branch, got[0]))

        def held(group):
            return pltpu.VMEM((len(group), height, LANES), jnp.int32)

        last, groups = last_group(size)
        early = [s for group in groups for s in group]
        first = call(
            functools.partial(early_kernel, groups, axis), partial, [VMEM] * (HALVES + len(early)), VMEM,
            [held(group) for group in groups], product // 2, (*branch, *(got[s] for s in early)))
        return call(
            functools.partial(kernel, last, 1, axis), out_shape, [VMEM] * (1 + HALVES + len(last)), out_specs,
            [held(last), *scratch], product // 2, (first, *branch, *(got[s] for s in last)))

    size = lax.axis_size("narrow")
    shapes = coded("narrow")
    whole = jax.ShapeDtypeStruct(branches.shape[1:], jnp.float32)
    meets = jax.ShapeDtypeStruct((columns, columns), jnp.bfloat16)
    meets_rows = jax.ShapeDtypeStruct((mode_order.shape[0] - 1, SUBLANES, columns), jnp.int32)
    stem_scratch = [order, pltpu.VMEM(local.shape, jnp.float32)]
    if size > DIRECT:
        out, rows_of_meets = call(
            functools.partial(whole_kernel, "narrow"), [*shapes, meets_rows], [HBM] * 3, [VMEM] * 2,
            [*stem_scratch, pltpu.VMEM(whole.shape, jnp.float32), arrays("narrow"), pltpu.SemaphoreType.DMA((4,))],
            product, (mode_order, local, branches))
        got = swap([out], "narrow")
        second_raw, second_meets, third_meets = call(
            meets_kernel, [whole, meets, meets], [VMEM, HBM], [VMEM] * 3,
            [pltpu.SemaphoreType.DMA], columns**2, (rows_of_meets, branches))
    else:
        half_blocks = pltpu.VMEM((size // 2, *block("narrow")[1:]), jnp.int32)
        *outs, rows_of_meets, moved, near = call(
            functools.partial(far_kernel, "narrow"),
            shapes[: size // 2]
            + [meets_rows, jax.ShapeDtypeStruct((4 * rows, columns), jnp.bfloat16)]
            + [jax.ShapeDtypeStruct((2, columns, part), jnp.float32)],
            [HBM] * 3, [VMEM] * (size // 2 + 3),
            [*stem_scratch, pltpu.VMEM((2, columns, part), jnp.float32), half_blocks, pltpu.SemaphoreType.DMA((5,))],
            product // 2, (mode_order, local, branches))
        order_of = partners(size)
        got = {s: send(out, s, "narrow") for s, out in zip([s for s in order_of if s >= size // 2], outs)}
        *outs, second_raw, second_meets, third_meets = call(
            functools.partial(near_kernel, "narrow"), shapes[: size // 2] + [whole, meets, meets],
            [VMEM, VMEM, VMEM, HBM], [VMEM] * (size // 2 + 3), [half_blocks, pltpu.SemaphoreType.DMA],
            product // 2, (moved, near, rows_of_meets, branches))
        for s, out in zip([s for s in order_of if s < size // 2], outs):
            got[s] = send(out, s, "narrow") if s else out
    *second_branch, third_raw = call(
        second_branch_kernel, [ready] * HALVES + [whole], [VMEM, VMEM, HBM], [VMEM] * (HALVES + 1),
        [pltpu.SemaphoreType.DMA], 8 * columns**3, (second_meets, second_raw, branches))
    shapes = coded("wide")
    outs = contracted(
        lambda group, early, axis, *refs: middle_kernel(group, early, axis, "wide", *refs),
        "narrow", second_branch, got, shapes, [VMEM] * len(shapes), [arrays("wide")])
    third_branch = call(
        third_branch_kernel, [ready] * HALVES, [ANY, VMEM, VMEM], [VMEM] * HALVES, [], 8 * columns**3,
        (outs[0], third_meets, third_raw))
    got = swap(outs, "wide")
    final = contracted(
        last_kernel, "wide", third_branch, got, jax.ShapeDtypeStruct((2, columns, rows), jnp.float32), HBM,
        [pltpu.VMEM((HALVES, 2, part, rows), jnp.float32), pltpu.SemaphoreType.DMA((2 * HALVES,))])
    return final.reshape(2, 1, 1, columns, rows)


def solution(mesh):
    return jax.shard_map(
        body,
        mesh=mesh,
        in_specs=(P(None, "wide", "narrow", None, None), P(), P()),
        out_specs=P(None, "wide", "narrow", None, None),
        check_vma=False,
    )
```

```python
import functools

import jax
import jax.numpy as jnp
from jax import lax
from jax.experimental import pallas as pl
from jax.experimental.pallas import tpu as pltpu
from jax.sharding import PartitionSpec as P

LANES = 128
SUBLANES = 8
TOP = 32766.0
FINE = 65536.0
HALVES = 2
DIRECT = 8
VMEM_LIMIT = 24 << 20


def split_pair(values):
    high = values.astype(jnp.bfloat16)
    low = (values - high.astype(jnp.float32)).astype(jnp.bfloat16)
    return high, low


def dot(left, right):
    return lax.dot_general(left, right, (((1,), (0,)), ((), ())), preferred_element_type=jnp.float32)


def meets_row(order_ref, step, columns):
    row = lax.broadcasted_iota(jnp.int32, (SUBLANES, columns), 1)
    meets = jnp.zeros_like(row)
    for b in range(order_ref.shape[1]):
        bit = jnp.bitwise_and(jnp.right_shift(row, order_ref[step, b]), 1)
        meets = meets + jnp.left_shift(bit, b)
    return meets


def one_hot(meets):
    columns = meets.shape[1]
    column = lax.broadcasted_iota(jnp.int32, (columns, columns), 0)
    return jnp.where(column == meets[0:1, :], 1.0, 0.0).astype(jnp.bfloat16)


def operands(pieces):
    real_high, imag_high, real_low, imag_low = pieces
    plain = jnp.concatenate([real_high, imag_high, real_low, imag_low], axis=0)
    turned = jnp.concatenate([-imag_high, real_high, -imag_low, real_low], axis=0)
    return plain, turned


def contract(plain, turned, high, low):
    rows = plain.shape[0] // 2
    left = jnp.concatenate([plain, turned], axis=1)
    both = dot(left, high)
    return both[:rows] + both[rows:] + dot(left[:rows], low)


def lane_block(shape, width):
    return lax.broadcasted_iota(jnp.int32, shape, 1) // width


def rotate(values, amount):
    amount = amount % LANES
    return pltpu.roll(values, amount, 1) if amount else values


def encode(out_ref, slot, real, imag):
    rows = real.shape[0]
    tall = jnp.maximum(jnp.abs(real), jnp.abs(imag)).reshape(rows // SUBLANES, SUBLANES, LANES)
    largest = jnp.maximum(jnp.max(tall, axis=0), 1e-30)
    level = jnp.ceil(jnp.log2(largest) * FINE)
    gain = jnp.exp2(level * (-1.0 / FINE)) * TOP
    gain = jnp.broadcast_to(gain[None], tall.shape).reshape(rows, LANES)
    upper = jnp.round(real * gain).astype(jnp.int32)
    lower = jnp.round(imag * gain).astype(jnp.int32)
    out_ref[slot, 0:rows, :] = jnp.bitwise_or(jnp.left_shift(upper, 16), jnp.bitwise_and(lower, 0xFFFF))
    out_ref[slot, rows : rows + SUBLANES, :] = level.astype(jnp.int32)


def decode(in_ref, slot):
    rows = in_ref.shape[1] - SUBLANES
    codes = in_ref[slot, 0:rows, :]
    level = in_ref[slot, rows : rows + SUBLANES, :].astype(jnp.float32)
    step = jnp.exp2(level * (1.0 / FINE)) * (1.0 / TOP)
    step = jnp.broadcast_to(step[None], (rows // SUBLANES, SUBLANES, LANES)).reshape(rows, LANES)
    real = jnp.right_shift(codes, 16).astype(jnp.float32) * step
    imag = jnp.right_shift(jnp.left_shift(codes, 16), 16).astype(jnp.float32) * step
    return real, imag


def pack(out_ref, tile, width, real, imag):
    share = LANES // width
    height = real.shape[0] // share
    for p in range(share):
        made = []
        for values in (real, imag):
            piece = rotate(values[0:height], -p * width)
            for q in range(1, share):
                other = rotate(values[q * height : (q + 1) * height], (q - p) * width)
                piece = jnp.where(lane_block(other.shape, width) == q, other, piece)
            made.append(piece)
        encode(out_ref, tile * share + p, *made)


def unpack(in_ref, columns):
    blocks = in_ref.shape[0]
    width = columns // blocks
    share = LANES // width
    tiles = []
    for tile in range(columns // LANES):
        got = [decode(in_ref, tile * share + p) for p in range(share)]
        both = []
        for c in range(2):
            groups = []
            for q in range(share):
                piece = rotate(got[0][c], -q * width)
                for p in range(1, share):
                    other = rotate(got[p][c], (p - q) * width)
                    piece = jnp.where(lane_block(other.shape, width) == p, other, piece)
                groups.append(piece)
            both.append(jnp.concatenate(groups, axis=0) if share > 1 else groups[0])
        tiles.append(both)
    return tuple(jnp.concatenate([t[c] for t in tiles], axis=1) for c in range(2))


def partners(size):
    half = size // 2
    far = sorted(range(half, size), key=lambda s: (-(s % 2), s if size > 4 else -s))
    near = sorted(range(1, half), key=lambda s: (s > 1, -s))
    return [0, *far, *near]


PAIRINGS = (
    (5, 2, 1, 4, 3, 0, 7, 6),
    (3, 7, 6, 0, 5, 4, 2, 1),
    (6, 4, 3, 2, 1, 7, 0, 5),
    (7, 3, 4, 1, 2, 6, 5, 0),
    (1, 0, 5, 7, 6, 2, 4, 3),
    (4, 6, 7, 5, 0, 3, 1, 2),
    (2, 5, 0, 6, 7, 1, 3, 4),
)


def paired(axis):
    return axis == "wide" and lax.axis_size(axis) == len(PAIRINGS) + 1


def travel_plan(axis):
    size = lax.axis_size(axis)
    if paired(axis):
        return [tuple(range(size)), *PAIRINGS]
    return [tuple(i ^ s for i in range(size)) for s in partners(size)]


def partner(row, me):
    found = jnp.int32(row[0])
    for i, other in enumerate(row[1:], 1):
        found = jnp.where(me == i, jnp.int32(other), found)
    return found


def early_blocks(axis):
    size = lax.axis_size(axis)
    if paired(axis):
        return list(range(size - 2))
    return [k for k, row in enumerate(travel_plan(axis)) if row[0] < size // 2]


def exchange_ready(out_refs, chunks, axis):
    if len(out_refs) == 1:
        out_refs[0][...] = chunks[...]
        return
    me = lax.axis_index(axis)
    for row, ref in zip(travel_plan(axis), out_refs):
        ref[...] = chunks[partner(row, me)]


def copies_of_stem(order_hbm, stem_hbm, order_ref, stem_ref, sems):
    copies = [pltpu.make_async_copy(order_hbm, order_ref, sems.at[0])]
    copies += [pltpu.make_async_copy(stem_hbm.at[c], stem_ref.at[c], sems.at[1 + c]) for c in range(2)]
    for copy in copies:
        copy.start()
    return copies


def relabelled_stem(order_ref, stem_ref, copies):
    copies[0].wait()
    meets = one_hot(meets_row(order_ref, 0, stem_ref.shape[1]))
    for copy in copies[1:]:
        copy.wait()
    rows = stem_ref.shape[2]
    moved = [
        dot(jnp.concatenate(split_pair(stem_ref[c].T), axis=0), meets).astype(jnp.bfloat16) for c in range(2)
    ]
    return jnp.concatenate([moved[0][:rows], moved[1][:rows], moved[0][rows:], moved[1][rows:]], axis=0)


def four(pieces):
    rows = pieces.shape[0] // 4
    return operands([pieces[q * rows : (q + 1) * rows] for q in range(4)])


def pack_all(chunks, first, width, sums):
    rows = sums.shape[0] // 2
    for tile in range(sums.shape[1] // LANES):
        lanes = slice(tile * LANES, (tile + 1) * LANES)
        pack(chunks, first + tile, width, sums[:rows, lanes], sums[rows:, lanes])


def keep_meets(order_ref, meets_ref):
    for step in range(1, order_ref.shape[0]):
        meets_ref[step - 1] = meets_row(order_ref, step, meets_ref.shape[2])


def whole_kernel(axis, order_hbm, stem_hbm, branches_hbm, out_ref, meets_ref, order_ref, stem_ref, held, chunks, sems):
    columns = held.shape[1]
    copies = copies_of_stem(order_hbm, stem_hbm, order_ref, stem_ref, sems)
    copy = pltpu.make_async_copy(branches_hbm.at[0], held, sems.at[3])
    copy.start()
    plain, turned = four(relabelled_stem(order_ref, stem_ref, copies))
    copy.wait()
    high, low = split_pair(held[...].reshape(2 * columns, columns))
    pack_all(chunks, 0, columns // chunks.shape[0], contract(plain, turned, high, low))
    exchange_ready((out_ref,), chunks, axis)
    keep_meets(order_ref, meets_ref)


def far_kernel(axis, order_hbm, stem_hbm, branches_hbm, *refs):
    *out_refs, meets_ref, moved_ref, near_ref, order_ref, stem_ref, held, chunks, sems = refs
    columns, part = held.shape[1:]
    size = 2 * len(out_refs)
    me = lax.axis_index(axis)
    near = pl.multiple_of(me // (size // 2) * part, part)
    far = pl.multiple_of((1 - me // (size // 2)) * part, part)
    copies = copies_of_stem(order_hbm, stem_hbm, order_ref, stem_ref, sems)
    copy = pltpu.make_async_copy(branches_hbm.at[0, :, :, pl.ds(far, part)], held, sems.at[3])
    near_copy = pltpu.make_async_copy(branches_hbm.at[0, :, :, pl.ds(near, part)], near_ref, sems.at[4])
    copy.start()
    near_copy.start()
    moved = relabelled_stem(order_ref, stem_ref, copies)
    moved_ref[...] = moved
    plain, turned = four(moved)
    copy.wait()
    high, low = split_pair(held[...].reshape(2 * columns, part))
    pack_all(chunks, 0, columns // size, contract(plain, turned, high, low))
    for s, ref in zip([s for s in partners(size) if s >= size // 2], out_refs):
        ref[...] = chunks[jnp.bitwise_and(jnp.bitwise_xor(me, s), size // 2 - 1)]
    keep_meets(order_ref, meets_ref)
    near_copy.wait()


def near_kernel(axis, moved_ref, near_ref, meets_ref, branches_hbm, *refs):
    *out_refs, next_ref, second_meets, third_meets, chunks, sem = refs
    columns, part = near_ref.shape[1:]
    size = 2 * len(out_refs)
    me = lax.axis_index(axis)
    next_copy = pltpu.make_async_copy(branches_hbm.at[1], next_ref, sem)
    next_copy.start()
    plain, turned = four(moved_ref[...])
    high, low = split_pair(near_ref[...].reshape(2 * columns, part))
    pack_all(chunks, 0, columns // size, contract(plain, turned, high, low))
    for s, ref in zip([s for s in partners(size) if s < size // 2], out_refs):
        ref[...] = chunks[jnp.bitwise_and(jnp.bitwise_xor(me, s), size // 2 - 1)]
    second_meets[...] = one_hot(meets_ref[0])
    third_meets[...] = one_hot(meets_ref[1])
    next_copy.wait()


def meets_kernel(meets_ref, branches_hbm, next_ref, second_meets, third_meets, sem):
    next_copy = pltpu.make_async_copy(branches_hbm.at[1], next_ref, sem)
    next_copy.start()
    second_meets[...] = one_hot(meets_ref[0])
    third_meets[...] = one_hot(meets_ref[1])
    next_copy.wait()


def relabel(meets_ref, from_ref, to_refs):
    part = to_refs[0].shape[2]
    for h, to_ref in enumerate(to_refs):
        for c in range(2):
            high, low = split_pair(from_ref[c, :, h * part : (h + 1) * part])
            to_ref[c] = dot(meets_ref[...], high).astype(jnp.bfloat16)
            to_ref[2 + c] = dot(meets_ref[...], low).astype(jnp.bfloat16)


def second_branch_kernel(meets_ref, from_ref, branches_hbm, *refs):
    *to_refs, next_ref, sem = refs
    copy = pltpu.make_async_copy(branches_hbm.at[2], next_ref, sem)
    copy.start()
    relabel(meets_ref, from_ref, to_refs)
    copy.wait()


def third_branch_kernel(after_ref, meets_ref, from_ref, *to_refs):
    relabel(meets_ref, from_ref, to_refs)


def received(in_refs, blocks, axis, chunks, columns):
    firsts = []
    if axis is None:
        chunks[...] = in_refs[0][...]
        firsts.append((0, columns))
    else:
        plan = travel_plan(axis)
        width = columns // len(blocks)
        me = lax.axis_index(axis)
        for slot, (k, ref) in enumerate(zip(blocks, in_refs)):
            chunks[slot] = ref[...]
            firsts.append((pl.multiple_of(partner(plan[k], me) * width, width), width))
    real, imag = unpack(chunks, columns)
    real_high, real_low = split_pair(real)
    imag_high, imag_low = split_pair(imag)
    return *operands((real_high, imag_high, real_low, imag_low)), firsts


def rows_of(branch_ref, firsts):
    def rows(pieces):
        return jnp.concatenate([branch_ref[q, pl.ds(first, width), :] for q in pieces for first, width in firsts], axis=0)

    return rows((0, 1)), rows((2, 3))


def early_kernel(blocks, axis, *refs):
    branch_refs, in_refs, (out_ref, chunks) = refs[:HALVES], refs[HALVES:-2], refs[-2:]
    part = branch_refs[0].shape[2]
    columns = branch_refs[0].shape[1] // lax.axis_size(axis) * len(blocks)
    plain, turned, firsts = received(in_refs, blocks, axis, chunks, columns)
    for h, ref in enumerate(branch_refs):
        out_ref[:, h * part : (h + 1) * part] = contract(plain, turned, *rows_of(ref, firsts))


def late_sums(blocks, early, axis, refs, chunks):
    sums_ref, refs = (refs[0], refs[1:]) if early else (None, refs)
    branch_refs, in_refs = refs[:HALVES], refs[HALVES:]
    columns = branch_refs[0].shape[1]
    if early:
        columns = columns // lax.axis_size(axis) * len(blocks)
    plain, turned, firsts = received(in_refs, blocks, axis, chunks, columns)
    part = branch_refs[0].shape[2]
    for h, ref in enumerate(branch_refs):
        sums = contract(plain, turned, *rows_of(ref, firsts))
        yield h, part, sums + sums_ref[:, h * part : (h + 1) * part] if early else sums


def middle_kernel(group, early, in_axis, out_axis, *refs):
    ins = early + HALVES + len(group)
    out_refs, (arrived, chunks) = refs[ins:-2], refs[-2:]
    for h, part, sums in late_sums(group, early, in_axis, refs[:ins], arrived):
        pack_all(chunks, h * (part // LANES), part * HALVES // chunks.shape[0], sums)
    exchange_ready(out_refs, chunks, out_axis)


def last_kernel(group, early, in_axis, *refs):
    ins = early + HALVES + len(group)
    out_hbm, arrived, done, sems = refs[ins:]
    copies = []
    for h, part, sums in late_sums(group, early, in_axis, refs[:ins], arrived):
        rows = sums.shape[0] // 2
        for c in range(2):
            done[h, c] = sums[c * rows : (c + 1) * rows].T
            copy = pltpu.make_async_copy(done.at[h, c], out_hbm.at[c, pl.ds(h * part, part), :], sems.at[2 * h + c])
            copy.start()
            copies.append(copy)
    for copy in copies:
        copy.wait()


def send(out, k, axis):
    return lax.ppermute(out, axis, list(enumerate(travel_plan(axis)[k]))) if k else out


def swap(outs, axis):
    if lax.axis_size(axis) > DIRECT:
        return [lax.all_to_all(outs[0], axis, split_axis=0, concat_axis=0, tiled=True)]
    return [send(out, k, axis) for k, out in enumerate(outs)]


HBM = pl.BlockSpec(memory_space=pltpu.HBM)
VMEM = pl.BlockSpec(memory_space=pltpu.VMEM)
ANY = pl.BlockSpec(memory_space=pl.ANY)


def call(kernel, out_shape, in_specs, out_specs, scratch, flops, args):
    params = pltpu.CompilerParams(vmem_limit_bytes=VMEM_LIMIT)
    cost = pl.CostEstimate(flops=flops, bytes_accessed=4 << 20, transcendentals=0)
    return pl.pallas_call(
        kernel, out_shape=out_shape, in_specs=in_specs, out_specs=out_specs, scratch_shapes=scratch,
        compiler_params=params, cost_estimate=cost,
    )(*args)


def body(stem, branches, mode_order):
    columns, rows = stem.shape[3:]
    part = columns // HALVES

    def block(axis):
        size = lax.axis_size(axis)
        return size, rows * columns // size // LANES + SUBLANES, LANES

    def coded(axis):
        shape = block(axis)
        if shape[0] > DIRECT:
            return [jax.ShapeDtypeStruct(shape, jnp.int32)]
        return [jax.ShapeDtypeStruct(shape[1:], jnp.int32)] * shape[0]

    def arrays(axis):
        return pltpu.VMEM(block(axis), jnp.int32)

    branches = pltpu.with_memory_space_constraint(branches, pltpu.HBM)
    mode_order = pltpu.with_memory_space_constraint(mode_order, pltpu.HBM)
    local = pltpu.with_memory_space_constraint(stem.reshape(2, columns, rows), pltpu.HBM)
    order = pltpu.SMEM(mode_order.shape, jnp.int32)
    product = 24 * rows * columns * columns

    ready = jax.ShapeDtypeStruct((4, columns, part), jnp.bfloat16)
    partial = jax.ShapeDtypeStruct((2 * rows, columns), jnp.float32)

    def contracted(kernel, axis, branch, got, out_shape, out_specs, scratch):
        size, height, _ = block(axis)
        if size > DIRECT:
            return call(
                functools.partial(kernel, (0,), 0, None), out_shape, [VMEM] * (HALVES + 1), out_specs,
                [arrays(axis), *scratch], product, (*branch, got[0]))

        early = early_blocks(axis)
        late = [k for k in range(size) if k not in early]
        first, last = (pltpu.VMEM((len(blocks), height, LANES), jnp.int32) for blocks in (early, late))
        sums = call(
            functools.partial(early_kernel, early, axis), partial, [VMEM] * (HALVES + len(early)), VMEM, [first],
            product // 2, (*branch, *(got[k] for k in early)))
        return call(
            functools.partial(kernel, late, 1, axis), out_shape, [VMEM] * (1 + HALVES + len(late)), out_specs,
            [last, *scratch], product // 2, (sums, *branch, *(got[k] for k in late)))

    size = lax.axis_size("narrow")
    shapes = coded("narrow")
    whole = jax.ShapeDtypeStruct(branches.shape[1:], jnp.float32)
    meets = jax.ShapeDtypeStruct((columns, columns), jnp.bfloat16)
    meets_rows = jax.ShapeDtypeStruct((mode_order.shape[0] - 1, SUBLANES, columns), jnp.int32)
    stem_scratch = [order, pltpu.VMEM(local.shape, jnp.float32)]
    if size > DIRECT:
        out, rows_of_meets = call(
            functools.partial(whole_kernel, "narrow"), [*shapes, meets_rows], [HBM] * 3, [VMEM] * 2,
            [*stem_scratch, pltpu.VMEM(whole.shape, jnp.float32), arrays("narrow"), pltpu.SemaphoreType.DMA((4,))],
            product, (mode_order, local, branches))
        got = swap([out], "narrow")
        second_raw, second_meets, third_meets = call(
            meets_kernel, [whole, meets, meets], [VMEM, HBM], [VMEM] * 3,
            [pltpu.SemaphoreType.DMA], columns**2, (rows_of_meets, branches))
    else:
        half_blocks = pltpu.VMEM((size // 2, *block("narrow")[1:]), jnp.int32)
        *outs, rows_of_meets, moved, near_half = call(
            functools.partial(far_kernel, "narrow"),
            shapes[: size // 2]
            + [meets_rows, jax.ShapeDtypeStruct((4 * rows, columns), jnp.bfloat16)]
            + [jax.ShapeDtypeStruct((2, columns, part), jnp.float32)],
            [HBM] * 3, [VMEM] * (size // 2 + 3),
            [*stem_scratch, pltpu.VMEM((2, columns, part), jnp.float32), half_blocks, pltpu.SemaphoreType.DMA((5,))],
            product // 2, (mode_order, local, branches))
        near = early_blocks("narrow")
        far = [k for k in range(size) if k not in near]
        got = dict(zip(far, (send(out, k, "narrow") for k, out in zip(far, outs))))
        *outs, second_raw, second_meets, third_meets = call(
            functools.partial(near_kernel, "narrow"), shapes[: size // 2] + [whole, meets, meets],
            [VMEM, VMEM, VMEM, HBM], [VMEM] * (size // 2 + 3), [half_blocks, pltpu.SemaphoreType.DMA],
            product // 2, (moved, near_half, rows_of_meets, branches))
        got.update(zip(near, (send(out, k, "narrow") for k, out in zip(near, outs))))
    *second_branch, third_raw = call(
        second_branch_kernel, [ready] * HALVES + [whole], [VMEM, VMEM, HBM], [VMEM] * (HALVES + 1),
        [pltpu.SemaphoreType.DMA], 8 * columns**3, (second_meets, second_raw, branches))
    shapes = coded("wide")
    outs = contracted(
        lambda group, early, axis, *refs: middle_kernel(group, early, axis, "wide", *refs),
        "narrow", second_branch, got, shapes, [VMEM] * len(shapes), [arrays("wide")])
    third_branch = call(
        third_branch_kernel, [ready] * HALVES, [ANY, VMEM, VMEM], [VMEM] * HALVES, [], 8 * columns**3,
        (outs[0], third_meets, third_raw))
    got = swap(outs, "wide")
    final = contracted(
        last_kernel, "wide", third_branch, got, jax.ShapeDtypeStruct((2, columns, rows), jnp.float32), HBM,
        [pltpu.VMEM((HALVES, 2, part, rows), jnp.float32), pltpu.SemaphoreType.DMA((2 * HALVES,))])
    return final.reshape(2, 1, 1, columns, rows)


def solution(mesh):
    return jax.shard_map(
        body,
        mesh=mesh,
        in_specs=(P(None, "wide", "narrow", None, None), P(), P()),
        out_specs=P(None, "wide", "narrow", None, None),
        check_vma=False,
    )
```

```python
import functools

import jax
import jax.numpy as jnp
from jax import lax
from jax.experimental import pallas as pl
from jax.experimental.pallas import tpu as pltpu
from jax.sharding import PartitionSpec as P

LANES = 128
SUBLANES = 8
TOP = 32700.0
FINE = 65536.0
HALVES = 2
DIRECT = 8
VMEM_LIMIT = 24 << 20


def split_pair(values):
    high = values.astype(jnp.bfloat16)
    low = (values - high.astype(jnp.float32)).astype(jnp.bfloat16)
    return high, low


def dot(left, right):
    return lax.dot_general(left, right, (((1,), (0,)), ((), ())), preferred_element_type=jnp.float32)


def meets_row(order_ref, step, columns):
    row = lax.broadcasted_iota(jnp.int32, (SUBLANES, columns), 1)
    meets = jnp.zeros_like(row)
    for b in range(order_ref.shape[1]):
        bit = jnp.bitwise_and(jnp.right_shift(row, order_ref[step, b]), 1)
        meets = meets + jnp.left_shift(bit, b)
    return meets


def one_hot(meets):
    columns = meets.shape[1]
    column = lax.broadcasted_iota(jnp.int32, (columns, columns), 0)
    return jnp.where(column == meets[0:1, :], 1.0, 0.0).astype(jnp.bfloat16)


def operands(pieces):
    real_high, imag_high, real_low, imag_low = pieces
    plain = jnp.concatenate([real_high, imag_high, real_low, imag_low], axis=0)
    turned = jnp.concatenate([-imag_high, real_high, -imag_low, real_low], axis=0)
    return plain, turned


def contract(plain, turned, high, low):
    rows = plain.shape[0] // 2
    left = jnp.concatenate([plain, turned], axis=1)
    both = dot(left, high)
    return both[:rows] + both[rows:] + dot(left[:rows], low)


def lane_block(shape, width):
    return lax.broadcasted_iota(jnp.int32, shape, 1) // width


def rotate(values, amount):
    amount = amount % LANES
    return pltpu.roll(values, amount, 1) if amount else values


def encode(out_ref, slot, real, imag):
    rows = real.shape[0]
    tall = jnp.maximum(jnp.abs(real), jnp.abs(imag)).reshape(rows // SUBLANES, SUBLANES, LANES)
    largest = jnp.maximum(jnp.max(tall, axis=0), 1e-30)
    level = jnp.ceil(jnp.log2(largest) * FINE)
    gain = jnp.exp2(level * (-1.0 / FINE)) * TOP
    gain = jnp.broadcast_to(gain[None], tall.shape).reshape(rows, LANES)
    upper = jnp.round(real * gain).astype(jnp.int32)
    lower = jnp.round(imag * gain).astype(jnp.int32)
    out_ref[slot, 0:rows, :] = jnp.bitwise_or(jnp.left_shift(upper, 16), jnp.bitwise_and(lower, 0xFFFF))
    out_ref[slot, rows : rows + SUBLANES, :] = level.astype(jnp.int32)


def decode(in_ref, slot):
    rows = in_ref.shape[1] - SUBLANES
    codes = in_ref[slot, 0:rows, :]
    level = in_ref[slot, rows : rows + SUBLANES, :].astype(jnp.float32)
    step = jnp.exp2(level * (1.0 / FINE)) * (1.0 / TOP)
    step = jnp.broadcast_to(step[None], (rows // SUBLANES, SUBLANES, LANES)).reshape(rows, LANES)
    real = jnp.right_shift(codes, 16).astype(jnp.float32) * step
    imag = jnp.right_shift(jnp.left_shift(codes, 16), 16).astype(jnp.float32) * step
    return real, imag


def pack(out_ref, tile, width, real, imag):
    share = LANES // width
    height = real.shape[0] // share
    for p in range(share):
        made = []
        for values in (real, imag):
            piece = rotate(values[0:height], -p * width)
            for q in range(1, share):
                other = rotate(values[q * height : (q + 1) * height], (q - p) * width)
                piece = jnp.where(lane_block(other.shape, width) == q, other, piece)
            made.append(piece)
        encode(out_ref, tile * share + p, *made)


def unpack(in_ref, columns):
    blocks = in_ref.shape[0]
    width = columns // blocks
    share = LANES // width
    tiles = []
    for tile in range(columns // LANES):
        got = [decode(in_ref, tile * share + p) for p in range(share)]
        both = []
        for c in range(2):
            groups = []
            for q in range(share):
                piece = rotate(got[0][c], -q * width)
                for p in range(1, share):
                    other = rotate(got[p][c], (p - q) * width)
                    piece = jnp.where(lane_block(other.shape, width) == p, other, piece)
                groups.append(piece)
            both.append(jnp.concatenate(groups, axis=0) if share > 1 else groups[0])
        tiles.append(both)
    return tuple(jnp.concatenate([t[c] for t in tiles], axis=1) for c in range(2))


def partners(size):
    half = size // 2
    far = sorted(range(half, size), key=lambda s: (-(s % 2), s if size > 4 else -s))
    near = sorted(range(1, half), key=lambda s: (s > 1, -s))
    return [0, *far, *near]


PAIRINGS = (
    (5, 2, 1, 4, 3, 0, 7, 6),
    (3, 7, 6, 0, 5, 4, 2, 1),
    (6, 4, 3, 2, 1, 7, 0, 5),
    (7, 3, 4, 1, 2, 6, 5, 0),
    (1, 0, 5, 7, 6, 2, 4, 3),
    (4, 6, 7, 5, 0, 3, 1, 2),
    (2, 5, 0, 6, 7, 1, 3, 4),
)


def paired(axis):
    return axis == "wide" and lax.axis_size(axis) == len(PAIRINGS) + 1


def travel_plan(axis):
    size = lax.axis_size(axis)
    if paired(axis):
        return [tuple(range(size)), *PAIRINGS]
    return [tuple(i ^ s for i in range(size)) for s in partners(size)]


def partner(row, me):
    found = jnp.int32(row[0])
    for i, other in enumerate(row[1:], 1):
        found = jnp.where(me == i, jnp.int32(other), found)
    return found


def early_blocks(axis):
    size = lax.axis_size(axis)
    if paired(axis):
        return list(range(size - 2))
    return [k for k, row in enumerate(travel_plan(axis)) if row[0] < size // 2]


def exchange_ready(out_refs, chunks, axis):
    if len(out_refs) == 1:
        out_refs[0][...] = chunks[...]
        return
    me = lax.axis_index(axis)
    for row, ref in zip(travel_plan(axis), out_refs):
        ref[...] = chunks[partner(row, me)]


def copies_of_stem(order_hbm, stem_hbm, order_ref, stem_ref, sems):
    copies = [pltpu.make_async_copy(order_hbm, order_ref, sems.at[0])]
    copies += [pltpu.make_async_copy(stem_hbm.at[c], stem_ref.at[c], sems.at[1 + c]) for c in range(2)]
    for copy in copies:
        copy.start()
    return copies


def relabelled_stem(order_ref, stem_ref, copies):
    copies[0].wait()
    meets = one_hot(meets_row(order_ref, 0, stem_ref.shape[1]))
    for copy in copies[1:]:
        copy.wait()
    rows = stem_ref.shape[2]
    moved = [
        dot(jnp.concatenate(split_pair(stem_ref[c].T), axis=0), meets).astype(jnp.bfloat16) for c in range(2)
    ]
    return jnp.concatenate([moved[0][:rows], moved[1][:rows], moved[0][rows:], moved[1][rows:]], axis=0)


def four(pieces):
    rows = pieces.shape[0] // 4
    return operands([pieces[q * rows : (q + 1) * rows] for q in range(4)])


def pack_all(chunks, first, width, sums):
    rows = sums.shape[0] // 2
    for tile in range(sums.shape[1] // LANES):
        lanes = slice(tile * LANES, (tile + 1) * LANES)
        pack(chunks, first + tile, width, sums[:rows, lanes], sums[rows:, lanes])


def keep_meets(order_ref, meets_ref):
    for step in range(1, order_ref.shape[0]):
        meets_ref[step - 1] = meets_row(order_ref, step, meets_ref.shape[2])


def whole_kernel(axis, order_hbm, stem_hbm, branches_hbm, out_ref, meets_ref, order_ref, stem_ref, held, chunks, sems):
    columns = held.shape[1]
    copies = copies_of_stem(order_hbm, stem_hbm, order_ref, stem_ref, sems)
    copy = pltpu.make_async_copy(branches_hbm.at[0], held, sems.at[3])
    copy.start()
    plain, turned = four(relabelled_stem(order_ref, stem_ref, copies))
    copy.wait()
    high, low = split_pair(held[...].reshape(2 * columns, columns))
    pack_all(chunks, 0, columns // chunks.shape[0], contract(plain, turned, high, low))
    exchange_ready((out_ref,), chunks, axis)
    keep_meets(order_ref, meets_ref)


def far_kernel(axis, order_hbm, stem_hbm, branches_hbm, *refs):
    *out_refs, meets_ref, moved_ref, near_ref, order_ref, stem_ref, held, chunks, sems = refs
    columns, part = held.shape[1:]
    size = 2 * len(out_refs)
    me = lax.axis_index(axis)
    near = pl.multiple_of(me // (size // 2) * part, part)
    far = pl.multiple_of((1 - me // (size // 2)) * part, part)
    copies = copies_of_stem(order_hbm, stem_hbm, order_ref, stem_ref, sems)
    copy = pltpu.make_async_copy(branches_hbm.at[0, :, :, pl.ds(far, part)], held, sems.at[3])
    near_copy = pltpu.make_async_copy(branches_hbm.at[0, :, :, pl.ds(near, part)], near_ref, sems.at[4])
    copy.start()
    near_copy.start()
    moved = relabelled_stem(order_ref, stem_ref, copies)
    moved_ref[...] = moved
    plain, turned = four(moved)
    copy.wait()
    high, low = split_pair(held[...].reshape(2 * columns, part))
    pack_all(chunks, 0, columns // size, contract(plain, turned, high, low))
    for s, ref in zip([s for s in partners(size) if s >= size // 2], out_refs):
        ref[...] = chunks[jnp.bitwise_and(jnp.bitwise_xor(me, s), size // 2 - 1)]
    keep_meets(order_ref, meets_ref)
    near_copy.wait()


def near_kernel(axis, moved_ref, near_ref, meets_ref, branches_hbm, *refs):
    *out_refs, next_ref, second_meets, third_meets, chunks, sem = refs
    columns, part = near_ref.shape[1:]
    size = 2 * len(out_refs)
    me = lax.axis_index(axis)
    next_copy = pltpu.make_async_copy(branches_hbm.at[1], next_ref, sem)
    next_copy.start()
    plain, turned = four(moved_ref[...])
    high, low = split_pair(near_ref[...].reshape(2 * columns, part))
    pack_all(chunks, 0, columns // size, contract(plain, turned, high, low))
    for s, ref in zip([s for s in partners(size) if s < size // 2], out_refs):
        ref[...] = chunks[jnp.bitwise_and(jnp.bitwise_xor(me, s), size // 2 - 1)]
    second_meets[...] = one_hot(meets_ref[0])
    third_meets[...] = one_hot(meets_ref[1])
    next_copy.wait()


def meets_kernel(meets_ref, branches_hbm, next_ref, second_meets, third_meets, sem):
    next_copy = pltpu.make_async_copy(branches_hbm.at[1], next_ref, sem)
    next_copy.start()
    second_meets[...] = one_hot(meets_ref[0])
    third_meets[...] = one_hot(meets_ref[1])
    next_copy.wait()


def relabel(meets_ref, from_ref, to_refs):
    part = to_refs[0].shape[2]
    for h, to_ref in enumerate(to_refs):
        for c in range(2):
            high, low = split_pair(from_ref[c, :, h * part : (h + 1) * part])
            to_ref[c] = dot(meets_ref[...], high).astype(jnp.bfloat16)
            to_ref[2 + c] = dot(meets_ref[...], low).astype(jnp.bfloat16)


def second_branch_kernel(meets_ref, from_ref, branches_hbm, *refs):
    *to_refs, next_ref, sem = refs
    copy = pltpu.make_async_copy(branches_hbm.at[2], next_ref, sem)
    copy.start()
    relabel(meets_ref, from_ref, to_refs)
    copy.wait()


def third_branch_kernel(after_ref, meets_ref, from_ref, *to_refs):
    relabel(meets_ref, from_ref, to_refs)


def received(in_refs, blocks, axis, chunks, columns):
    firsts = []
    if axis is None:
        chunks[...] = in_refs[0][...]
        firsts.append((0, columns))
    else:
        plan = travel_plan(axis)
        width = columns // len(blocks)
        me = lax.axis_index(axis)
        for slot, (k, ref) in enumerate(zip(blocks, in_refs)):
            chunks[slot] = ref[...]
            firsts.append((pl.multiple_of(partner(plan[k], me) * width, width), width))
    real, imag = unpack(chunks, columns)
    real_high, real_low = split_pair(real)
    imag_high, imag_low = split_pair(imag)
    return *operands((real_high, imag_high, real_low, imag_low)), firsts


def rows_of(branch_ref, firsts):
    def rows(pieces):
        return jnp.concatenate([branch_ref[q, pl.ds(first, width), :] for q in pieces for first, width in firsts], axis=0)

    return rows((0, 1)), rows((2, 3))


def early_kernel(blocks, axis, *refs):
    branch_refs, in_refs, (out_ref, chunks) = refs[:HALVES], refs[HALVES:-2], refs[-2:]
    part = branch_refs[0].shape[2]
    columns = branch_refs[0].shape[1] // lax.axis_size(axis) * len(blocks)
    plain, turned, firsts = received(in_refs, blocks, axis, chunks, columns)
    for h, ref in enumerate(branch_refs):
        out_ref[:, h * part : (h + 1) * part] = contract(plain, turned, *rows_of(ref, firsts))


def late_sums(blocks, early, axis, refs, chunks):
    sums_ref, refs = (refs[0], refs[1:]) if early else (None, refs)
    branch_refs, in_refs = refs[:HALVES], refs[HALVES:]
    columns = branch_refs[0].shape[1]
    if early:
        columns = columns // lax.axis_size(axis) * len(blocks)
    plain, turned, firsts = received(in_refs, blocks, axis, chunks, columns)
    part = branch_refs[0].shape[2]
    for h, ref in enumerate(branch_refs):
        sums = contract(plain, turned, *rows_of(ref, firsts))
        yield h, part, sums + sums_ref[:, h * part : (h + 1) * part] if early else sums


def middle_kernel(group, early, in_axis, out_axis, *refs):
    ins = early + HALVES + len(group)
    out_refs, (arrived, chunks) = refs[ins:-2], refs[-2:]
    for h, part, sums in late_sums(group, early, in_axis, refs[:ins], arrived):
        pack_all(chunks, h * (part // LANES), part * HALVES // chunks.shape[0], sums)
    exchange_ready(out_refs, chunks, out_axis)


def last_kernel(group, early, in_axis, *refs):
    ins = early + HALVES + len(group)
    out_hbm, arrived, done, sems = refs[ins:]
    copies = []
    for h, part, sums in late_sums(group, early, in_axis, refs[:ins], arrived):
        rows = sums.shape[0] // 2
        for c in range(2):
            done[h, c] = sums[c * rows : (c + 1) * rows].T
            copy = pltpu.make_async_copy(done.at[h, c], out_hbm.at[c, pl.ds(h * part, part), :], sems.at[2 * h + c])
            copy.start()
            copies.append(copy)
    for copy in copies:
        copy.wait()


def send(out, k, axis):
    return lax.ppermute(out, axis, list(enumerate(travel_plan(axis)[k]))) if k else out


def swap(outs, axis):
    if lax.axis_size(axis) > DIRECT:
        return [lax.all_to_all(outs[0], axis, split_axis=0, concat_axis=0, tiled=True)]
    return [send(out, k, axis) for k, out in enumerate(outs)]


HBM = pl.BlockSpec(memory_space=pltpu.HBM)
VMEM = pl.BlockSpec(memory_space=pltpu.VMEM)
ANY = pl.BlockSpec(memory_space=pl.ANY)


def call(kernel, out_shape, in_specs, out_specs, scratch, flops, args):
    params = pltpu.CompilerParams(vmem_limit_bytes=VMEM_LIMIT)
    cost = pl.CostEstimate(flops=flops, bytes_accessed=4 << 20, transcendentals=0)
    return pl.pallas_call(
        kernel, out_shape=out_shape, in_specs=in_specs, out_specs=out_specs, scratch_shapes=scratch,
        compiler_params=params, cost_estimate=cost,
    )(*args)


def body(stem, branches, mode_order):
    columns, rows = stem.shape[3:]
    part = columns // HALVES

    def block(axis):
        size = lax.axis_size(axis)
        return size, rows * columns // size // LANES + SUBLANES, LANES

    def coded(axis):
        shape = block(axis)
        if shape[0] > DIRECT:
            return [jax.ShapeDtypeStruct(shape, jnp.int32)]
        return [jax.ShapeDtypeStruct(shape[1:], jnp.int32)] * shape[0]

    def arrays(axis):
        return pltpu.VMEM(block(axis), jnp.int32)

    branches = pltpu.with_memory_space_constraint(branches, pltpu.HBM)
    mode_order = pltpu.with_memory_space_constraint(mode_order, pltpu.HBM)
    local = pltpu.with_memory_space_constraint(stem.reshape(2, columns, rows), pltpu.HBM)
    order = pltpu.SMEM(mode_order.shape, jnp.int32)
    product = 24 * rows * columns * columns

    ready = jax.ShapeDtypeStruct((4, columns, part), jnp.bfloat16)
    partial = jax.ShapeDtypeStruct((2 * rows, columns), jnp.float32)

    def contracted(kernel, axis, branch, got, out_shape, out_specs, scratch):
        size, height, _ = block(axis)
        if size > DIRECT:
            return call(
                functools.partial(kernel, (0,), 0, None), out_shape, [VMEM] * (HALVES + 1), out_specs,
                [arrays(axis), *scratch], product, (*branch, got[0]))

        early = early_blocks(axis)
        late = [k for k in range(size) if k not in early]
        first, last = (pltpu.VMEM((len(blocks), height, LANES), jnp.int32) for blocks in (early, late))
        sums = call(
            functools.partial(early_kernel, early, axis), partial, [VMEM] * (HALVES + len(early)), VMEM, [first],
            product // 2, (*branch, *(got[k] for k in early)))
        return call(
            functools.partial(kernel, late, 1, axis), out_shape, [VMEM] * (1 + HALVES + len(late)), out_specs,
            [last, *scratch], product // 2, (sums, *branch, *(got[k] for k in late)))

    size = lax.axis_size("narrow")
    shapes = coded("narrow")
    whole = jax.ShapeDtypeStruct(branches.shape[1:], jnp.float32)
    meets = jax.ShapeDtypeStruct((columns, columns), jnp.bfloat16)
    meets_rows = jax.ShapeDtypeStruct((mode_order.shape[0] - 1, SUBLANES, columns), jnp.int32)
    stem_scratch = [order, pltpu.VMEM(local.shape, jnp.float32)]
    if size > DIRECT:
        out, rows_of_meets = call(
            functools.partial(whole_kernel, "narrow"), [*shapes, meets_rows], [HBM] * 3, [VMEM] * 2,
            [*stem_scratch, pltpu.VMEM(whole.shape, jnp.float32), arrays("narrow"), pltpu.SemaphoreType.DMA((4,))],
            product, (mode_order, local, branches))
        got = swap([out], "narrow")
        second_raw, second_meets, third_meets = call(
            meets_kernel, [whole, meets, meets], [VMEM, HBM], [VMEM] * 3,
            [pltpu.SemaphoreType.DMA], columns**2, (rows_of_meets, branches))
    else:
        half_blocks = pltpu.VMEM((size // 2, *block("narrow")[1:]), jnp.int32)
        *outs, rows_of_meets, moved, near_half = call(
            functools.partial(far_kernel, "narrow"),
            shapes[: size // 2]
            + [meets_rows, jax.ShapeDtypeStruct((4 * rows, columns), jnp.bfloat16)]
            + [jax.ShapeDtypeStruct((2, columns, part), jnp.float32)],
            [HBM] * 3, [VMEM] * (size // 2 + 3),
            [*stem_scratch, pltpu.VMEM((2, columns, part), jnp.float32), half_blocks, pltpu.SemaphoreType.DMA((5,))],
            product // 2, (mode_order, local, branches))
        near = early_blocks("narrow")
        far = [k for k in range(size) if k not in near]
        got = dict(zip(far, (send(out, k, "narrow") for k, out in zip(far, outs))))
        *outs, second_raw, second_meets, third_meets = call(
            functools.partial(near_kernel, "narrow"), shapes[: size // 2] + [whole, meets, meets],
            [VMEM, VMEM, VMEM, HBM], [VMEM] * (size // 2 + 3), [half_blocks, pltpu.SemaphoreType.DMA],
            product // 2, (moved, near_half, rows_of_meets, branches))
        got.update(zip(near, (send(out, k, "narrow") for k, out in zip(near, outs))))
    *second_branch, third_raw = call(
        second_branch_kernel, [ready] * HALVES + [whole], [VMEM, VMEM, HBM], [VMEM] * (HALVES + 1),
        [pltpu.SemaphoreType.DMA], 8 * columns**3, (second_meets, second_raw, branches))
    shapes = coded("wide")
    outs = contracted(
        lambda group, early, axis, *refs: middle_kernel(group, early, axis, "wide", *refs),
        "narrow", second_branch, got, shapes, [VMEM] * len(shapes), [arrays("wide")])
    third_branch = call(
        third_branch_kernel, [ready] * HALVES, [ANY, VMEM, VMEM], [VMEM] * HALVES, [], 8 * columns**3,
        (outs[0], third_meets, third_raw))
    got = swap(outs, "wide")
    final = contracted(
        last_kernel, "wide", third_branch, got, jax.ShapeDtypeStruct((2, columns, rows), jnp.float32), HBM,
        [pltpu.VMEM((HALVES, 2, part, rows), jnp.float32), pltpu.SemaphoreType.DMA((2 * HALVES,))])
    return final.reshape(2, 1, 1, columns, rows)


def solution(mesh):
    return jax.shard_map(
        body,
        mesh=mesh,
        in_specs=(P(None, "wide", "narrow", None, None), P(), P()),
        out_specs=P(None, "wide", "narrow", None, None),
        check_vma=False,
    )
```
